512 devices in a mesh: rep: 64 (over z, y_lo, x), fsdp: 8 (over y_hi, core).
Axes of the slice: x: 4, y: 8 (y_hi: 4, y_lo: 2; y = y_hi * 2 + y_lo), z: 8, core: 2. Of those that a mesh axis runs over, the one named last changes fastest.
Arguments:
- deltas: bfloat16 [64, 57344, 128], P('rep', 'fsdp'), may hold values from -1 to 1
- scales: bfloat16 [64, 57344], P('rep', 'fsdp'), may hold values from 0.1 to 30, as said below
- clip_level: float32 [], replicated, may hold values from 0.02 to 0.05
- master: float32 [57344, 128], P(('fsdp', 'rep')), may hold values from -6 to 6
- momentum: float32 [57344, 128], P(('fsdp', 'rep')), may hold values from -0.75 to 0.75
Outputs:
- new_base: bfloat16 [256, 28672], P('fsdp')
- new_master: float32 [57344, 128], P(('fsdp', 'rep'))
- new_momentum: float32 [57344, 128], P(('fsdp', 'rep'))
The draws below stay inside these ranges and needn't reach their ends.
Inputs may be any that keep to these rules, and one draw needn't show every extreme that they name: `scales`: positive.
All inputs are finite; a program needn't handle non-finite values.
Results may differ from the reference program's by a relative error of at most 0.0004.
Values may be sent and summed in bfloat16 or wider, within the bound.
A program may use at most 64 MiB of HBM per device.

```python
import jax
import jax.numpy as jnp
from jax import lax

FF = 28672
QBLOCK = 128
REPLICAS = 64
ROWS = 256
BLOCKS = 57344


def draw_scales(key, part):
    levels = jax.random.uniform(key, (REPLICAS, BLOCKS), jnp.float32)
    growth = 1.0 + 2.0 * jnp.arange(BLOCKS, dtype=jnp.float32) / BLOCKS
    return (0.2 * 10.0 ** (1.5 * levels) * growth[None, :]).astype(jnp.bfloat16)


def block_scale(own_key, extent, pieces, smallest, high):
    level, own = 1.0, jax.random.fold_in(own_key, 6)
    for position, parts in pieces:
        heights = jnp.exp(jax.random.uniform(jax.random.fold_in(own, position), (parts,), jnp.float32, smallest / len(pieces), high / len(pieces)))
        level = level * jnp.repeat(heights, extent[position] // parts).reshape([-1 if axis == position else 1 for axis in range(len(extent))])
    return level


def gaussian(rng, dims, scale, most, shards=(), kind=jnp.bfloat16):
    result = scale * jax.random.normal(rng, dims, jnp.float32)
    if shards:
        result = result * block_scale(rng, dims, shards, -0.22, 0.18)
    return jnp.clip(result, -most, most).astype(kind)


def setup_inputs(seed: int = 0) -> dict:
    key_list = jax.random.split(jax.random.key(seed), 6)
    return {
        "deltas": jnp.clip(jax.random.uniform(key_list[0], (REPLICAS, BLOCKS, QBLOCK), jnp.float32, -1.0, 1.0) * block_scale(key_list[0], (REPLICAS, BLOCKS, QBLOCK), ((0, 64), (1, 8)), -0.4, 0.0), -1.0, 1.0).astype(jnp.bfloat16),
        "scales": draw_scales(jax.random.fold_in(key_list[5], 71), 0),
        "clip_level": jnp.clip(jax.random.uniform(key_list[2], (), jnp.float32, 0.02, 0.05), 0.02, 0.05),
        "master": gaussian(key_list[3], (BLOCKS, QBLOCK), 1.0, 6.0, ((0, 512),), jnp.float32),
        "momentum": gaussian(key_list[4], (BLOCKS, QBLOCK), 0.05, 0.75, ((0, 512),), jnp.float32),
    }


def reference(deltas, scales, clip_level, master, momentum):

    def accumulate(running, slices):
        values, factors = slices
        return (running + values.astype(jnp.float32) * factors.astype(jnp.float32)[:, None], None)
    start_sum = jnp.zeros((BLOCKS, QBLOCK), jnp.float32)
    summed, _ = lax.scan(accumulate, start_sum, (deltas, scales))
    outer_grad = summed / REPLICAS
    mean_square = jnp.mean(outer_grad * outer_grad)
    factor = jnp.minimum(1.0, clip_level / jnp.sqrt(mean_square + 1e-06))
    new_momentum = 0.9 * momentum + factor * outer_grad
    new_master = master - 0.7 * (factor * outer_grad + 0.9 * new_momentum)
    new_base = new_master.astype(jnp.bfloat16).reshape(ROWS, FF)
    return (new_base, new_master, new_momentum)
```

```python
import functools

import jax
import jax.numpy as jnp
from jax import lax
from jax.experimental import pallas as pl
from jax.experimental.pallas import tpu as pltpu
from jax.sharding import PartitionSpec as P

FF = 28672
MESH = pl.DeviceIdType.MESH
NX, NY, NZ = 4, 2, 8
ROWS = 112
PAD = 128
ORDER = (4, 3, 5, 2, 6, 1, 7, 0)
BF16, F32 = jnp.bfloat16, jnp.float32


def kernel(
    deltas, scales, clip, master, momentum,
    gathered, grad_out, factor_out,
    rx, table, table16, rs, sf, ysrc, yrx, zsrc, zrx, acc, a_own, az, gz, nb, sq, ar_rx,
    local_sem, xs, xr, ss, sr, ys, yr, zs, zr, as_, ar, gs, gr, qs, qr, bs, br,
):
    rep, fsdp = lax.axis_index("rep"), lax.axis_index("fsdp")
    x, yl, z = lax.rem(rep, 4), lax.rem(rep // 4, 2), rep // 8
    yh, core = fsdp // 2, lax.rem(fsdp, 2)
    y = yh * 2 + yl

    def device(x, yl, z):
        return ((z * 2 + yl) * 4 + x, fsdp)

    def along_x(d):
        return device(lax.rem(x + d, 4), yl, z)

    def along_z(d):
        return device(x, yl, lax.rem(z + d, 8))

    y_peer = device(x, 1 - yl, z)

    def along_xc(d):
        other = lax.rem(core + d // 4, 2)
        return ((z * 2 + yl) * 4 + lax.rem(x + d % 4, 4), yh * 2 + other)

    def along_y(d):
        to = lax.rem(y + d, 8)
        return ((z * 2 + lax.rem(to, 2)) * 4 + x, (to // 2) * 2 + core)

    barrier = pltpu.get_barrier_semaphore()
    for d in range(1, 8):
        for peer in (along_z(d), along_xc(d), along_y(d)):
            pl.semaphore_signal(barrier, inc=1, device_id=peer, device_id_type=MESH)

    own = pltpu.make_async_copy(deltas.at[:, x], rx.at[:, x, pl.ds(0, ROWS)], local_sem)
    own.start()
    a_own[...] = master[...] - 0.567 * momentum[...]
    pl.semaphore_wait(barrier, 21)

    def remote(src, dst, send, recv, to):
        copy = pltpu.make_async_remote_copy(
            src_ref=src, dst_ref=dst, send_sem=send, recv_sem=recv, device_id=to, device_id_type=MESH
        )
        copy.start()
        return copy

    xcopies = []
    for s, dz in enumerate(ORDER):
        to = lax.rem(z + dz, 8)
        copies = []
        for k, d in enumerate((2, 1, 3)):
            xd = lax.rem(x + d, 4)
            copies.append(
                remote(
                    deltas.at[pl.ds(2 * to, 2), xd], rx.at[pl.ds(2 * to, 2), x, pl.ds(0, ROWS)],
                    xs.at[s, k], xr.at[s, k], along_x(d),
                )
            )
        xcopies.append(copies)
        if s == 0:
            flat = scales[...].astype(F32)
            for r in range(NX * NY * NZ):
                table[r % 4, r // 4 : r // 4 + 1, 0:ROWS] = flat[:, ROWS * r : ROWS * (r + 1)]
            for k in range(4):
                table16[k] = table[k].astype(BF16)
            scopies = [
                remote(table16.at[lax.rem(x + d, 4)], rs.at[x], ss.at[k], sr.at[k], along_x(d))
                for k, d in enumerate((2, 1, 3))
            ]
    acopies = [remote(a_own, az.at[z], as_.at[d - 1], ar.at[d - 1], along_z(d)) for d in range(1, 8)]

    for zy in range(16):
        for k in range(4):
            rx[zy, k, ROWS:PAD] = jnp.zeros((PAD - ROWS, 128), BF16)
    for copy in scopies:
        copy.wait()
    for k in range(4):
        sf[k] = rs[k].astype(F32)
    sf[x] = table[x]
    own.wait()

    eye = lax.broadcasted_iota(jnp.int32, (ROWS, PAD), 0) == lax.broadcasted_iota(jnp.int32, (ROWS, PAD), 1)

    def decode(zy):
        diags = [
            jnp.where(eye, jnp.broadcast_to(sf[k, pl.ds(zy, 1), :], (ROWS, PAD)), 0.0).astype(BF16)
            for k in range(4)
        ]
        return jnp.dot(
            jnp.concatenate(diags, axis=1), rx[zy].reshape(4 * PAD, 128), preferred_element_type=F32
        )

    ycopies, zcopies = [], []

    def finish(s):
        ycopies[s].wait()
        total = acc[s] + yrx[s]
        if ORDER[s] == 0:
            acc[s] = total
        else:
            zsrc[s] = total
            zcopies.append(
                remote(zsrc.at[s], zrx.at[s], zs.at[s], zr.at[s], along_z(ORDER[s]))
            )

    for s, dz in enumerate(ORDER):
        to = lax.rem(z + dz, 8)
        for copy in xcopies[s]:
            copy.wait()
        ysrc[s] = decode(2 * to + 1 - yl)
        ycopies.append(remote(ysrc.at[s], yrx.at[s], ys.at[s], yr.at[s], y_peer))
        acc[s] = decode(2 * to + yl)
        if s > 0:
            finish(s - 1)
    finish(7)
    total = acc[7]
    for s in range(7):
        zcopies[s].wait()
        total = total + zrx[s]
    grad = total * (1.0 / (NX * NY * NZ))
    grad_out[...] = grad
    gz[z] = grad
    partial = jnp.sum((grad * grad).reshape(ROWS // 8, 8, 128), axis=0)
    sq[0] = partial
    gcopies = None
    for stage, way in enumerate((along_xc, along_y, along_z)):
        copies = [
            remote(sq.at[stage], ar_rx.at[stage, d - 1], qs.at[stage, d - 1], qr.at[stage, d - 1], way(d))
            for d in range(1, 8)
        ]
        if gcopies is None:
            gcopies = [remote(gz.at[z], gz.at[z], gs.at[d - 1], gr.at[d - 1], along_z(d)) for d in range(1, 8)]
        for d in range(7):
            copies[d].wait()
            partial = partial + ar_rx[stage, d]
        if stage < 2:
            sq[stage + 1] = partial
    mean = jnp.sum(jnp.sum(partial, axis=1, keepdims=True), axis=0, keepdims=True) * (1.0 / (512 * ROWS * 128))
    factor = jnp.minimum(1.0, clip[0, 0] / jnp.sqrt(mean + 1e-06))
    factor_out[...] = jnp.broadcast_to(factor, (8, 128))
    for copy in acopies + gcopies:
        copy.wait()
    az[z] = a_own[...]
    step = 1.33 * factor

    def send_base(zi, to, i):
        here = nb.at[zi]
        return remote(here, gathered.at[zi, yl, x], bs.at[i], br.at[i], to)

    first = []
    n = 0
    for zi in (0, 4, 1, 5, 2, 6, 3, 7):
        nb[zi] = (az[zi] - step * gz[zi]).astype(BF16)
        if zi < 4:
            for d in (2, 1, 3):
                first.append((zi, d, send_base(zi, along_x(d), n)))
                n += 1
        else:
            first.append((zi, 0, send_base(zi, y_peer, n)))
            n += 1
    second = []
    for zi in (0, 1, 2, 3):
        second.append(send_base(zi, y_peer, n))
        n += 1
        for d in (2, 1, 3):
            second.append(send_base(zi + 4, along_x(d), n))
            n += 1
    for zi, d, copy in first:
        copy.wait()
        if zi < 4:
            source = lax.rem(x + 4 - d, 4)
            block = gathered.at[zi, yl, source]
            second.append(remote(block, block, bs.at[n], br.at[n], y_peer))
            n += 1
        else:
            block = gathered.at[zi, 1 - yl, x]
            for d in (2, 1, 3):
                second.append(remote(block, block, bs.at[n], br.at[n], along_x(d)))
                n += 1
    whole = pltpu.make_async_copy(nb, gathered.at[:, yl, x], local_sem)
    whole.start()
    whole.wait()
    for copy in second:
        copy.wait()


def finish_kernel(gathered, grad, factor, master, momentum, base, new_master, new_momentum, wide):
    wide[...] = gathered[...].reshape(16 * ROWS, 128).astype(F32)
    for j in range(ROWS):
        base[:, 128 * j : 128 * (j + 1)] = wide[pl.ds(j, 16, stride=ROWS), :].astype(BF16)

    @pl.when((pl.program_id(0) == 0) & (pl.program_id(1) == 0))
    def _():
        scaled = factor[0:1, 0:1] * grad[...]
        moved = 0.9 * momentum[...] + scaled
        new_momentum[...] = moved
        new_master[...] = master[...] - 0.7 * (scaled + 0.9 * moved)


def per_device(deltas, scales, clip_level, master, momentum):
    vmem, anywhere = pl.BlockSpec(memory_space=pltpu.VMEM), pl.BlockSpec(memory_space=pl.ANY)
    dma = pltpu.SemaphoreType.DMA
    gathered, grad, factor = pl.pallas_call(
        kernel,
        out_shape=(
            jax.ShapeDtypeStruct((NZ, NY, NX, ROWS, 128), BF16),
            jax.ShapeDtypeStruct((ROWS, 128), F32),
            jax.ShapeDtypeStruct((8, 128), F32),
        ),
        in_specs=[anywhere, vmem, pl.BlockSpec(memory_space=pltpu.SMEM), vmem, vmem],
        out_specs=(anywhere, vmem, vmem),
        scratch_shapes=[
            pltpu.VMEM((NZ * NY, NX, PAD, 128), BF16),
            pltpu.VMEM((NX, NZ * NY, 128), F32),
            pltpu.VMEM((NX, NZ * NY, 128), BF16),
            pltpu.VMEM((NX, NZ * NY, 128), BF16),
            pltpu.VMEM((NX, NZ * NY, 128), F32),
            pltpu.VMEM((NZ, ROWS, 128), F32),
            pltpu.VMEM((NZ, ROWS, 128), F32),
            pltpu.VMEM((NZ, ROWS, 128), F32),
            pltpu.VMEM((NZ, ROWS, 128), F32),
            pltpu.VMEM((NZ, ROWS, 128), F32),
            pltpu.VMEM((ROWS, 128), F32),
            pltpu.VMEM((NZ, ROWS, 128), F32),
            pltpu.VMEM((NZ, ROWS, 128), F32),
            pltpu.VMEM((NZ, ROWS, 128), BF16),
            pltpu.VMEM((3, 8, 128), F32),
            pltpu.VMEM((3, 7, 8, 128), F32),
            dma,
            dma((8, 3)), dma((8, 3)),
            dma((3,)), dma((3,)),
            dma((8,)), dma((8,)),
            dma((8,)), dma((8,)),
            dma((7,)), dma((7,)),
            dma((7,)), dma((7,)),
            dma((3, 7)), dma((3, 7)),
            dma((56,)), dma((56,)),
        ],
        compiler_params=pltpu.CompilerParams(
            collective_id=0, has_side_effects=True, vmem_limit_bytes=40 * 2**20
        ),
    )(
        deltas.reshape(NZ * NY, NX, ROWS, 128), scales, clip_level.reshape(1, 1), master, momentum
    )
    small = lambda shape: pl.BlockSpec(shape, lambda h, i: (0, 0))
    return pl.pallas_call(
        finish_kernel,
        grid=(2, 2),
        out_shape=(
            jax.ShapeDtypeStruct((32, FF), BF16),
            jax.ShapeDtypeStruct((ROWS, 128), F32),
            jax.ShapeDtypeStruct((ROWS, 128), F32),
        ),
        in_specs=[
            pl.BlockSpec((16, None, ROWS, 128), lambda h, i: (i, h, 0, 0)),
            small((ROWS, 128)), small((8, 128)), small((ROWS, 128)), small((ROWS, 128)),
        ],
        out_specs=(
            pl.BlockSpec((16, FF // 2), lambda h, i: (i, h)), small((ROWS, 128)), small((ROWS, 128)),
        ),
        scratch_shapes=[pltpu.VMEM((16 * ROWS, 128), F32)],
    )(gathered.reshape(32, 2, ROWS, 128), grad, factor, master, momentum)


def solution(mesh):
    fr = ("fsdp", "rep")
    in_specs = (P("rep", "fsdp", None), P("rep", "fsdp"), P(), P(fr, None), P(fr, None))
    out_specs = (P("fsdp", None), P(fr, None), P(fr, None))
    return jax.shard_map(
        per_device, mesh=mesh, in_specs=in_specs, out_specs=out_specs, check_vma=False
    )
```

```python
import functools

import jax
import jax.numpy as jnp
from jax import lax
from jax.experimental import pallas as pl
from jax.experimental.pallas import tpu as pltpu
from jax.sharding import PartitionSpec as P

FF = 28672
MESH = pl.DeviceIdType.MESH
NX, NY, NZ = 4, 2, 8
ROWS = 112
PAD = 128
SEQUENCE = (
    (0, 4), (0, 3), (0, 5), (1, 4), (0, 2), (1, 3), (0, 6), (1, 5),
    (0, 1), (0, 7), (0, 0), (1, 2), (1, 6), (1, 1), (1, 7), (1, 0),
)
BF16, F32 = jnp.bfloat16, jnp.float32


def kernel(
    deltas, scales, clip, master, momentum,
    gathered, grad_out, factor_out,
    scales_v, clip_v, master_v, momentum_v, rx, table, table16, rs, sf, ysrc, yrx, zsrc, zrx, az, gz, nb, sq, ar_rx,
    own_sem, in_sem, xs, xr, ss, sr, ys, yr, zs, zr, as_, ar, gs, gr, qs, qr, bs, br,
):
    rep, fsdp = lax.axis_index("rep"), lax.axis_index("fsdp")
    x, yl, z = lax.rem(rep, 4), lax.rem(rep // 4, 2), rep // 8
    yh, core = fsdp // 2, lax.rem(fsdp, 2)
    y = yh * 2 + yl

    def device(x, yl, z):
        return ((z * 2 + yl) * 4 + x, fsdp)

    def along_x(d):
        return device(lax.rem(x + d, 4), yl, z)

    def along_z(d):
        return device(x, yl, lax.rem(z + d, 8))

    y_peer = device(x, 1 - yl, z)

    def along_xc(d):
        other = lax.rem(core + d // 4, 2)
        return ((z * 2 + yl) * 4 + lax.rem(x + d % 4, 4), yh * 2 + other)

    def along_y(d):
        to = lax.rem(y + d, 8)
        return ((z * 2 + lax.rem(to, 2)) * 4 + x, (to // 2) * 2 + core)

    barrier = pltpu.get_barrier_semaphore()
    for d in range(1, 8):
        for peer in (along_z(d), along_xc(d), along_y(d)):
            pl.semaphore_signal(barrier, inc=1, device_id=peer, device_id_type=MESH)

    own = pltpu.make_async_copy(deltas.at[:, x], rx.at[:, x, pl.ds(0, ROWS)], own_sem)
    own.start()
    inputs = [
        pltpu.make_async_copy(here, there, in_sem.at[i])
        for i, (here, there) in enumerate(
            ((scales, scales_v), (master, master_v), (momentum, momentum_v), (clip, clip_v))
        )
    ]
    for copy in inputs:
        copy.start()
    pl.semaphore_wait(barrier, 21)

    def remote(src, dst, send, recv, to):
        copy = pltpu.make_async_remote_copy(
            src_ref=src, dst_ref=dst, send_sem=send, recv_sem=recv, device_id=to, device_id_type=MESH
        )
        copy.start()
        return copy

    def chunk(mine, dz):
        return 2 * lax.rem(z + dz, 8) + (yl if mine else 1 - yl)

    xcopies = []
    for s, (mine, dz) in enumerate(SEQUENCE):
        zy = chunk(mine, dz)
        xcopies.append(
            [
                remote(
                    deltas.at[zy, lax.rem(x + d, 4)], rx.at[zy, x, pl.ds(0, ROWS)],
                    xs.at[s, k], xr.at[s, k], along_x(d),
                )
                for k, d in enumerate((2, 1, 3))
            ]
        )
        if s == 1:
            inputs[0].wait()
            flat = scales_v[...].astype(F32)
            for r in range(NX * NY * NZ):
                table[r % 4, r // 4 : r // 4 + 1, 0:ROWS] = flat[:, ROWS * r : ROWS * (r + 1)]
            for k in range(4):
                table16[k] = table[k].astype(BF16)
            scopies = [
                remote(table16.at[lax.rem(x + d, 4)], rs.at[x], ss.at[k], sr.at[k], along_x(d))
                for k, d in enumerate((2, 1, 3))
            ]

    def spread(blocks, send, recv):
        copies = []
        for i, d in enumerate((1, 7, 2, 6)):
            copies.append(remote(blocks.at[z], blocks.at[z], send.at[i], recv.at[i], along_z(d)))
        return copies

    def pass_on(blocks, send, recv, copies):
        for i, d in ((2, 2), (3, 6)):
            copies[i].wait()
            source = lax.rem(z + 8 - d, 8)
            block = blocks.at[source]
            copies.append(remote(block, block, send.at[i + 2], recv.at[i + 2], along_z(1 if d == 2 else 7)))
            half = blocks.at[source, pl.ds(0 if d == 2 else ROWS // 2, ROWS // 2)]
            copies.append(remote(half, half, send.at[i + 4], recv.at[i + 4], along_z(d)))
        return copies[:2] + copies[4:]

    inputs[1].wait()
    inputs[2].wait()
    az[z] = master_v[...] - 0.567 * momentum_v[...]
    acopies = spread(az, as_, ar)

    for zy in range(16):
        for k in range(4):
            rx[zy, k, ROWS:PAD] = jnp.zeros((PAD - ROWS, 128), BF16)
    for copy in scopies:
        copy.wait()
    for k in range(4):
        sf[k] = rs[k].astype(F32)
    sf[x] = table[x]
    own.wait()

    eye = lax.broadcasted_iota(jnp.int32, (ROWS, PAD), 0) == lax.broadcasted_iota(jnp.int32, (ROWS, PAD), 1)

    def decode(zy):
        diags = [
            jnp.where(eye, jnp.broadcast_to(sf[k, pl.ds(zy, 1), :], (ROWS, PAD)), 0.0).astype(BF16)
            for k in range(4)
        ]
        return jnp.dot(
            jnp.concatenate(diags, axis=1), rx[zy].reshape(4 * PAD, 128), preferred_element_type=F32
        )

    ycopies, zcopies = {}, []
    for s, (mine, dz) in enumerate(SEQUENCE):
        for copy in xcopies[s]:
            copy.wait()
        part = decode(chunk(mine, dz))
        if not mine:
            ysrc[dz] = part
            ycopies[dz] = remote(ysrc.at[dz], yrx.at[dz], ys.at[dz], yr.at[dz], y_peer)
        else:
            ycopies[dz].wait()
            total = part + yrx[dz]
            if dz:
                zsrc[dz - 1] = total
                zcopies.append(
                    remote(zsrc.at[dz - 1], zrx.at[dz - 1], zs.at[dz - 1], zr.at[dz - 1], along_z(dz))
                )
        if s == 5:
            acopies = pass_on(az, as_, ar, acopies)
    for copy in zcopies:
        copy.wait()
    for i in range(7):
        total = total + zrx[i]
    grad = total * (1.0 / (NX * NY * NZ))
    gz[z] = grad
    partial = jnp.sum((grad * grad).reshape(ROWS // 8, 8, 128), axis=0)
    sq[0] = partial
    for stage, way in enumerate((along_z, along_y, along_xc)):
        copies = [
            remote(sq.at[stage], ar_rx.at[stage, d - 1], qs.at[stage, d - 1], qr.at[stage, d - 1], way(d))
            for d in (4, 3, 5, 2, 6, 1, 7)
        ]
        if stage == 0:
            gcopies = spread(gz, gs, gr)
            grad_out[...] = grad
        elif stage == 1:
            gcopies = pass_on(gz, gs, gr, gcopies)
        for copy in copies:
            copy.wait()
        for d in range(7):
            partial = partial + ar_rx[stage, d]
        if stage == 0:
            sq[1] = partial
        elif stage == 1:
            sq[2] = partial
    mean = jnp.sum(jnp.sum(partial, axis=1, keepdims=True), axis=0, keepdims=True) * (1.0 / (512 * ROWS * 128))
    inputs[3].wait()
    factor = jnp.minimum(1.0, clip_v[...] / jnp.sqrt(mean + 1e-06))
    factor_out[...] = jnp.broadcast_to(factor, (8, 128))
    for copy in acopies + gcopies:
        copy.wait()
    step = 1.33 * factor

    counter = [0]

    def base_to(zi, yy, xx, to, src=None):
        n = counter[0]
        counter[0] += 1
        block = gathered.at[zi, yy, xx]
        return remote(block if src is None else src, block, bs.at[n], br.at[n], to)

    right, left = along_x(1), along_x(3)
    x_left, x_right = lax.rem(x + 3, 4), lax.rem(x + 1, 4)
    x_far = lax.rem(x + 2, 4)
    done, a_x, b_y = [], {}, {}
    for i in range(4):
        for zi in (i, i + 4):
            nb[zi] = (az[zi] - step * gz[zi]).astype(BF16)
        b_y[i + 4] = base_to(i + 4, yl, x, y_peer, nb.at[i + 4])
        a_x[i] = (
            base_to(i, yl, x, right, nb.at[i]), base_to(i, yl, x, left, nb.at[i]),
        )
    whole = pltpu.make_async_copy(nb, gathered.at[:, yl, x], own_sem)
    whole.start()
    b_x, b_x2, a_far, b_far = {}, {}, {}, {}
    for i in range(4):
        done.append(base_to(i, yl, x, y_peer, nb.at[i]))
        zi = i + 4
        b_x[zi] = (base_to(zi, yl, x, right, nb.at[zi]), base_to(zi, yl, x, left, nb.at[zi]))
    for i in range(4):
        from_left, from_right = a_x[i]
        from_left.wait()
        from_right.wait()
        if i % 2 == 0:
            a_far[i] = base_to(i, yl, x_left, right)
        else:
            a_far[i] = base_to(i, yl, x_right, left)
        done.append(base_to(i, yl, x_left, y_peer))
        done.append(base_to(i, yl, x_right, y_peer))
        zi = i + 4
        b_y[zi].wait()
        b_x2[zi] = (base_to(zi, 1 - yl, x, right), base_to(zi, 1 - yl, x, left))
    for i in range(4):
        a_far[i].wait()
        done.append(base_to(i, yl, x_far, y_peer))
        zi = i + 4
        for yy, pair in ((yl, b_x[zi]), (1 - yl, b_x2[zi])):
            for copy in pair:
                copy.wait()
            if i % 2 == 0:
                done.append(base_to(zi, yy, x_left, right))
            else:
                done.append(base_to(zi, yy, x_right, left))
    whole.wait()
    for copy in done:
        copy.wait()


def finish_kernel(
    gathered, grad, factor, master, momentum,
    base, new_master, new_momentum,
    blocks, rows, grad_v, factor_v, master_v, momentum_v, nm_v, nmom_v, in_sem, small_sem, out_sem,
):
    ins = [
        pltpu.make_async_copy(gathered.at[pl.ds(16 * i, 16), h], blocks.at[i, h], in_sem.at[i, h])
        for i in range(2) for h in range(2)
    ]
    smalls = [
        pltpu.make_async_copy(here, there, small_sem.at[i])
        for i, (here, there) in enumerate(
            ((grad, grad_v), (factor, factor_v), (master, master_v), (momentum, momentum_v))
        )
    ]
    for copy in smalls + ins:
        copy.start()
    for copy in smalls:
        copy.wait()
    scaled = factor_v[0:1, 0:1] * grad_v[...]
    moved = 0.9 * momentum_v[...] + scaled
    nmom_v[...] = moved
    nm_v[...] = master_v[...] - 0.7 * (scaled + 0.9 * moved)
    outs = [
        pltpu.make_async_copy(nm_v, new_master, out_sem.at[4]),
        pltpu.make_async_copy(nmom_v, new_momentum, out_sem.at[5]),
    ]
    for copy in outs:
        copy.start()
    for n in range(4):
        i, h = n // 2, n % 2
        ins[n].wait()
        for j in range(0, ROWS, 16):
            turned = jnp.swapaxes(blocks[i, h, :, j : j + 16, :], 0, 1)
            for k in range(16):
                rows[i, h, :, 128 * (j + k) : 128 * (j + k + 1)] = turned[k]
        out = pltpu.make_async_copy(
            rows.at[i, h], base.at[pl.ds(16 * i, 16), pl.ds(h * (FF // 2), FF // 2)], out_sem.at[n]
        )
        out.start()
        outs.append(out)
    for copy in outs:
        copy.wait()


def per_device(deltas, scales, clip_level, master, momentum):
    vmem, anywhere = pl.BlockSpec(memory_space=pltpu.VMEM), pl.BlockSpec(memory_space=pl.ANY)
    dma = pltpu.SemaphoreType.DMA
    gathered, grad, factor = pl.pallas_call(
        kernel,
        out_shape=(
            jax.ShapeDtypeStruct((NZ, NY, NX, ROWS, 128), BF16),
            jax.ShapeDtypeStruct((ROWS, 128), F32),
            jax.ShapeDtypeStruct((8, 128), F32),
        ),
        in_specs=[anywhere] * 5,
        out_specs=(anywhere, vmem, vmem),
        scratch_shapes=[
            pltpu.VMEM((1, NZ * NY * NX * ROWS), BF16),
            pltpu.VMEM((1, 1), F32),
            pltpu.VMEM((ROWS, 128), F32),
            pltpu.VMEM((ROWS, 128), F32),
            pltpu.VMEM((NZ * NY, NX, PAD, 128), BF16),
            pltpu.VMEM((NX, NZ * NY, 128), F32),
            pltpu.VMEM((NX, NZ * NY, 128), BF16),
            pltpu.VMEM((NX, NZ * NY, 128), BF16),
            pltpu.VMEM((NX, NZ * NY, 128), F32),
            pltpu.VMEM((NZ, ROWS, 128), F32),
            pltpu.VMEM((NZ, ROWS, 128), F32),
            pltpu.VMEM((NZ - 1, ROWS, 128), F32),
            pltpu.VMEM((NZ - 1, ROWS, 128), F32),
            pltpu.VMEM((NZ, ROWS, 128), F32),
            pltpu.VMEM((NZ, ROWS, 128), F32),
            pltpu.VMEM((NZ, ROWS, 128), BF16),
            pltpu.VMEM((3, 8, 128), F32),
            pltpu.VMEM((3, 7, 8, 128), F32),
            dma,
            dma((4,)),
            dma((16, 3)), dma((16, 3)),
            dma((3,)), dma((3,)),
            dma((8,)), dma((8,)),
            dma((7,)), dma((7,)),
            dma((8,)), dma((8,)),
            dma((8,)), dma((8,)),
            dma((3, 7)), dma((3, 7)),
            dma((56,)), dma((56,)),
        ],
        compiler_params=pltpu.CompilerParams(
            collective_id=0, has_side_effects=True, vmem_limit_bytes=60 * 2**20
        ),
    )(
        deltas.reshape(NZ * NY, NX, ROWS, 128), scales, clip_level.reshape(1, 1), master, momentum
    )
    half = FF // 2
    return pl.pallas_call(
        finish_kernel,
        out_shape=(
            jax.ShapeDtypeStruct((32, FF), BF16),
            jax.ShapeDtypeStruct((ROWS, 128), F32),
            jax.ShapeDtypeStruct((ROWS, 128), F32),
        ),
        in_specs=[anywhere] * 5,
        out_specs=(anywhere,) * 3,
        scratch_shapes=[
            pltpu.VMEM((2, 2, 16, ROWS, 128), BF16),
            pltpu.VMEM((2, 2, 16, half), BF16),
            pltpu.VMEM((ROWS, 128), F32),
            pltpu.VMEM((8, 128), F32),
            pltpu.VMEM((ROWS, 128), F32),
            pltpu.VMEM((ROWS, 128), F32),
            pltpu.VMEM((ROWS, 128), F32),
            pltpu.VMEM((ROWS, 128), F32),
            dma((2, 2)), dma((4,)), dma((6,)),
        ],
        compiler_params=pltpu.CompilerParams(vmem_limit_bytes=60 * 2**20),
    )(gathered.reshape(32, 2, ROWS, 128), grad, factor, master, momentum)


def solution(mesh):
    fr = ("fsdp", "rep")
    in_specs = (P("rep", "fsdp", None), P("rep", "fsdp"), P(), P(fr, None), P(fr, None))
    out_specs = (P("fsdp", None), P(fr, None), P(fr, None))
    return jax.shard_map(
        per_device, mesh=mesh, in_specs=in_specs, out_specs=out_specs, check_vma=False
    )
```

```python
import functools

import jax
import jax.numpy as jnp
from jax import lax
from jax.experimental import pallas as pl
from jax.experimental.pallas import tpu as pltpu
from jax.sharding import PartitionSpec as P

FF = 28672
MESH = pl.DeviceIdType.MESH
NX, NY, NZ = 4, 2, 8
ROWS = 112
PAD = 128
SEQUENCE = (
    (0, 4), (0, 3), (0, 5), (1, 4), (0, 2), (0, 6), (1, 3), (1, 5),
    (0, 1), (1, 2), (0, 7), (1, 6), (0, 0), (1, 1), (1, 7), (1, 0),
)
ALONG_ZC = tuple((0, 0, d, c) for c in (1, 0) for d in (4, 3, 5, 2, 6, 1, 7, 0))[:-1]
ALONG_YX = tuple((dx, d, 0, 0) for dx in (2, 1, 3, 0) for d in (4, 3, 5, 2, 6, 1, 7, 0))[:-1]
GREETED = (
    (1, 0, 0, 0), (2, 0, 0, 0), (3, 0, 0, 0), (0, 0, 0, 1), (0, 0, 1, 0), (0, 0, 2, 0), (0, 0, 6, 0), (0, 0, 7, 0),
    (0, 1, 0, 0), (0, 2, 0, 0), (0, 6, 0, 0), (0, 7, 0, 0),
)
BF16, F32 = jnp.bfloat16, jnp.float32


def kernel(
    deltas, scales, clip, master, momentum,
    gathered, grad_out, factor_out,
    scales_v, clip_v, master_v, momentum_v, rx, table, table16, rs, sf, ysrc, yrx, zsrc, zrx, az, gz, nb, sq, ar_rx,
    heard, own_sem, in_sem, xs, xr, ss, sr, ys, yr, zs, zr, as_, ar, gs, gr, qs, qr, bs, br,
):
    rep, fsdp = lax.axis_index("rep"), lax.axis_index("fsdp")
    x, yl, z = lax.rem(rep, 4), lax.rem(rep // 4, 2), rep // 8
    yh, core = fsdp // 2, lax.rem(fsdp, 2)
    y = yh * 2 + yl

    def device(x, yl, z):
        return ((z * 2 + yl) * 4 + x, fsdp)

    def along_x(d):
        return device(lax.rem(x + d, 4), yl, z)

    def along_z(d):
        return device(x, yl, lax.rem(z + d, 8))

    y_peer = device(x, 1 - yl, z)

    def partner(way):
        dx, dy, dz, dc = way
        to = lax.rem(y + dy, 8)
        return (
            (lax.rem(z + dz, 8) * 2 + lax.rem(to, 2)) * 4 + lax.rem(x + dx, 4),
            (to // 2) * 2 + lax.rem(core + dc, 2),
        )

    barrier = pltpu.get_barrier_semaphore()
    for way in GREETED:
        pl.semaphore_signal(barrier, inc=1, device_id=partner(way), device_id_type=MESH)

    own = pltpu.make_async_copy(deltas.at[:, x], rx.at[:, x, pl.ds(0, ROWS)], own_sem)
    own.start()
    inputs = [
        pltpu.make_async_copy(here, there, in_sem.at[i])
        for i, (here, there) in enumerate(
            ((scales, scales_v), (master, master_v), (momentum, momentum_v), (clip, clip_v))
        )
    ]
    for copy in inputs:
        copy.start()
    pl.semaphore_wait(barrier, len(GREETED))

    def remote(src, dst, send, recv, to):
        copy = pltpu.make_async_remote_copy(
            src_ref=src, dst_ref=dst, send_sem=send, recv_sem=recv, device_id=to, device_id_type=MESH
        )
        copy.start()
        return copy

    def chunk(mine, dz):
        return 2 * lax.rem(z + dz, 8) + (yl if mine else 1 - yl)

    xcopies = []
    for s, (mine, dz) in enumerate(SEQUENCE):
        zy = chunk(mine, dz)
        xcopies.append(
            [
                remote(
                    deltas.at[zy, lax.rem(x + d, 4)], rx.at[zy, x, pl.ds(0, ROWS)],
                    xs.at[s, k], xr.at[s, k], along_x(d),
                )
                for k, d in enumerate((2, 1, 3))
            ]
        )
        if s == 1:
            inputs[0].wait()
            flat = scales_v[...].astype(F32)
            for r in range(NX * NY * NZ):
                table[r % 4, r // 4 : r // 4 + 1, 0:ROWS] = flat[:, ROWS * r : ROWS * (r + 1)]
            for k in range(4):
                table16[k] = table[k].astype(BF16)
            scopies = [
                remote(table16.at[lax.rem(x + d, 4)], rs.at[x], ss.at[k], sr.at[k], along_x(d))
                for k, d in enumerate((2, 1, 3))
            ]

    def spread(blocks, send, recv):
        copies = []
        for i, d in enumerate((1, 7, 2, 6)):
            copies.append(remote(blocks.at[z], blocks.at[z], send.at[i], recv.at[i], along_z(d)))
        return copies

    def pass_on(blocks, send, recv, copies):
        for i, d in ((2, 2), (3, 6)):
            copies[i].wait()
            source = lax.rem(z + 8 - d, 8)
            block = blocks.at[source]
            copies.append(remote(block, block, send.at[i + 2], recv.at[i + 2], along_z(1 if d == 2 else 7)))
            half = blocks.at[source, pl.ds(0 if d == 2 else ROWS // 2, ROWS // 2)]
            copies.append(remote(half, half, send.at[i + 4], recv.at[i + 4], along_z(d)))
        return copies[:2] + copies[4:]

    inputs[1].wait()
    inputs[2].wait()
    az[z] = master_v[...] - 0.567 * momentum_v[...]
    acopies = spread(az, as_, ar)

    for zy in range(16):
        for k in range(4):
            rx[zy, k, ROWS:PAD] = jnp.zeros((PAD - ROWS, 128), BF16)
    for copy in scopies:
        copy.wait()
    for k in range(4):
        sf[k] = rs[k].astype(F32)
    sf[x] = table[x]
    own.wait()

    eye = lax.broadcasted_iota(jnp.int32, (ROWS, PAD), 0) == lax.broadcasted_iota(jnp.int32, (ROWS, PAD), 1)

    def decode(zy):
        diags = [
            jnp.where(eye, jnp.broadcast_to(sf[k, pl.ds(zy, 1), :], (ROWS, PAD)), 0.0).astype(BF16)
            for k in range(4)
        ]
        return jnp.dot(
            jnp.concatenate(diags, axis=1), rx[zy].reshape(4 * PAD, 128), preferred_element_type=F32
        )

    ycopies, zcopies = {}, {}
    for s, (mine, dz) in enumerate(SEQUENCE):
        for copy in xcopies[s]:
            copy.wait()
        part = decode(chunk(mine, dz))
        if not mine:
            ysrc[dz] = part
            ycopies[dz] = remote(ysrc.at[dz], yrx.at[dz], ys.at[dz], yr.at[dz], y_peer)
        else:
            ycopies[dz].wait()
            total = part + yrx[dz]
            before = {3: (4,), 2: (3,), 1: (2,), 6: (5,), 7: (6,), 0: (1, 7)}.get(dz, ())
            for far in before:
                zcopies[far].wait()
                total = total + zrx[far - 1]
            if dz:
                zsrc[dz - 1] = total
                zcopies[dz] = remote(
                    zsrc.at[dz - 1], zrx.at[dz - 1], zs.at[dz - 1], zr.at[dz - 1], along_z(1 if dz < 5 else 7)
                )
        if s == 5:
            acopies = pass_on(az, as_, ar, acopies)
        if s in (2, 7):
            if s == 7:
                pl.semaphore_wait(heard.at[0], 4)
            for d in (1, 2, 6, 7):
                pl.semaphore_signal(
                    heard.at[s // 7], inc=1, device_id=partner((0, d, 0, 0)), device_id_type=MESH
                )
    grad = total * (1.0 / (NX * NY * NZ))
    gz[z] = grad
    pl.semaphore_wait(heard.at[1], 4)
    partial = jnp.sum(grad * grad, axis=0, keepdims=True)
    for stage, ways in enumerate((ALONG_ZC, ALONG_YX)):
        first = stage * len(ALONG_ZC)
        sq[stage] = partial
        copies = [
            remote(sq.at[stage], ar_rx.at[first + i], qs.at[first + i], qr.at[first + i], partner(way))
            for i, way in enumerate(ways)
        ]
        if stage == 0:
            gcopies = spread(gz, gs, gr)
            grad_out[...] = grad
        else:
            gcopies = pass_on(gz, gs, gr, gcopies)
        for copy in copies:
            copy.wait()
        partial = partial + jnp.sum(ar_rx[first : first + len(ways)], axis=0)
    mean = jnp.sum(partial, axis=1, keepdims=True) * (1.0 / (512 * ROWS * 128))
    inputs[3].wait()
    factor = jnp.minimum(1.0, clip_v[...] / jnp.sqrt(mean + 1e-06))
    factor_out[...] = jnp.broadcast_to(factor, (8, 128))
    for copy in acopies + gcopies:
        copy.wait()
    step = 1.33 * factor

    counter = [0]

    def base_to(zi, yy, xx, to, src=None):
        n = counter[0]
        counter[0] += 1
        block = gathered.at[zi, yy, xx]
        return remote(block if src is None else src, block, bs.at[n], br.at[n], to)

    right, left = along_x(1), along_x(3)
    x_left, x_right = lax.rem(x + 3, 4), lax.rem(x + 1, 4)
    x_far = lax.rem(x + 2, 4)
    done, a_x, b_y = [], {}, {}
    for i in range(4):
        for zi in (i, i + 4):
            nb[zi] = (az[zi] - step * gz[zi]).astype(BF16)
        b_y[i + 4] = base_to(i + 4, yl, x, y_peer, nb.at[i + 4])
        a_x[i] = (
            base_to(i, yl, x, right, nb.at[i]), base_to(i, yl, x, left, nb.at[i]),
        )
    whole = pltpu.make_async_copy(nb, gathered.at[:, yl, x], own_sem)
    whole.start()
    b_x, b_x2, a_far, b_far = {}, {}, {}, {}
    for i in range(4):
        done.append(base_to(i, yl, x, y_peer, nb.at[i]))
        zi = i + 4
        b_x[zi] = (base_to(zi, yl, x, right, nb.at[zi]), base_to(zi, yl, x, left, nb.at[zi]))
    for i in range(4):
        from_left, from_right = a_x[i]
        from_left.wait()
        from_right.wait()
        if i % 2 == 0:
            a_far[i] = base_to(i, yl, x_left, right)
        else:
            a_far[i] = base_to(i, yl, x_right, left)
        done.append(base_to(i, yl, x_left, y_peer))
        done.append(base_to(i, yl, x_right, y_peer))
        zi = i + 4
        b_y[zi].wait()
        b_x2[zi] = (base_to(zi, 1 - yl, x, right), base_to(zi, 1 - yl, x, left))
    for i in range(4):
        a_far[i].wait()
        done.append(base_to(i, yl, x_far, y_peer))
        zi = i + 4
        for yy, pair in ((yl, b_x[zi]), (1 - yl, b_x2[zi])):
            for copy in pair:
                copy.wait()
            if i % 2 == 0:
                done.append(base_to(zi, yy, x_left, right))
            else:
                done.append(base_to(zi, yy, x_right, left))
    whole.wait()
    for copy in done:
        copy.wait()


def finish_kernel(
    gathered, grad, factor, master, momentum,
    base, new_master, new_momentum,
    blocks, rows, grad_v, factor_v, master_v, momentum_v, nm_v, nmom_v, in_sem, small_sem, out_sem,
):
    ins = [
        pltpu.make_async_copy(gathered.at[pl.ds(16 * i, 16), h], blocks.at[i, h], in_sem.at[i, h])
        for i in range(2) for h in range(2)
    ]
    smalls = [
        pltpu.make_async_copy(here, there, small_sem.at[i])
        for i, (here, there) in enumerate(
            ((grad, grad_v), (factor, factor_v), (master, master_v), (momentum, momentum_v))
        )
    ]
    for copy in smalls + ins:
        copy.start()
    for copy in smalls:
        copy.wait()
    scaled = factor_v[0:1, 0:1] * grad_v[...]
    moved = 0.9 * momentum_v[...] + scaled
    nmom_v[...] = moved
    nm_v[...] = master_v[...] - 0.7 * (scaled + 0.9 * moved)
    outs = [
        pltpu.make_async_copy(nm_v, new_master, out_sem.at[4]),
        pltpu.make_async_copy(nmom_v, new_momentum, out_sem.at[5]),
    ]
    for copy in outs:
        copy.start()
    for n in range(4):
        i, h = n // 2, n % 2
        ins[n].wait()
        for j in range(0, ROWS, 16):
            turned = jnp.swapaxes(blocks[i, h, :, j : j + 16, :], 0, 1)
            for k in range(16):
                rows[i, h, :, 128 * (j + k) : 128 * (j + k + 1)] = turned[k]
        out = pltpu.make_async_copy(
            rows.at[i, h], base.at[pl.ds(16 * i, 16), pl.ds(h * (FF // 2), FF // 2)], out_sem.at[n]
        )
        out.start()
        outs.append(out)
    for copy in outs:
        copy.wait()


def per_device(deltas, scales, clip_level, master, momentum):
    vmem, anywhere = pl.BlockSpec(memory_space=pltpu.VMEM), pl.BlockSpec(memory_space=pl.ANY)
    dma = pltpu.SemaphoreType.DMA
    gathered, grad, factor = pl.pallas_call(
        kernel,
        out_shape=(
            jax.ShapeDtypeStruct((NZ, NY, NX, ROWS, 128), BF16),
            jax.ShapeDtypeStruct((ROWS, 128), F32),
            jax.ShapeDtypeStruct((8, 128), F32),
        ),
        in_specs=[anywhere] * 5,
        out_specs=(anywhere, vmem, vmem),
        scratch_shapes=[
            pltpu.VMEM((1, NZ * NY * NX * ROWS), BF16),
            pltpu.VMEM((1, 1), F32),
            pltpu.VMEM((ROWS, 128), F32),
            pltpu.VMEM((ROWS, 128), F32),
            pltpu.VMEM((NZ * NY, NX, PAD, 128), BF16),
            pltpu.VMEM((NX, NZ * NY, 128), F32),
            pltpu.VMEM((NX, NZ * NY, 128), BF16),
            pltpu.VMEM((NX, NZ * NY, 128), BF16),
            pltpu.VMEM((NX, NZ * NY, 128), F32),
            pltpu.VMEM((NZ, ROWS, 128), F32),
            pltpu.VMEM((NZ, ROWS, 128), F32),
            pltpu.VMEM((NZ - 1, ROWS, 128), F32),
            pltpu.VMEM((NZ - 1, ROWS, 128), F32),
            pltpu.VMEM((NZ, ROWS, 128), F32),
            pltpu.VMEM((NZ, ROWS, 128), F32),
            pltpu.VMEM((NZ, ROWS, 128), BF16),
            pltpu.VMEM((2, 1, 128), F32),
            pltpu.VMEM((46, 1, 128), F32),
            pltpu.SemaphoreType.REGULAR((2,)),
            dma,
            dma((4,)),
            dma((16, 3)), dma((16, 3)),
            dma((3,)), dma((3,)),
            dma((8,)), dma((8,)),
            dma((7,)), dma((7,)),
            dma((8,)), dma((8,)),
            dma((8,)), dma((8,)),
            dma((46,)), dma((46,)),
            dma((56,)), dma((56,)),
        ],
        compiler_params=pltpu.CompilerParams(
            collective_id=0, has_side_effects=True, vmem_limit_bytes=60 * 2**20
        ),
    )(
        deltas.reshape(NZ * NY, NX, ROWS, 128), scales, clip_level.reshape(1, 1), master, momentum
    )
    half = FF // 2
    return pl.pallas_call(
        finish_kernel,
        out_shape=(
            jax.ShapeDtypeStruct((32, FF), BF16),
            jax.ShapeDtypeStruct((ROWS, 128), F32),
            jax.ShapeDtypeStruct((ROWS, 128), F32),
        ),
        in_specs=[anywhere] * 5,
        out_specs=(anywhere,) * 3,
        scratch_shapes=[
            pltpu.VMEM((2, 2, 16, ROWS, 128), BF16),
            pltpu.VMEM((2, 2, 16, half), BF16),
            pltpu.VMEM((ROWS, 128), F32),
            pltpu.VMEM((8, 128), F32),
            pltpu.VMEM((ROWS, 128), F32),
            pltpu.VMEM((ROWS, 128), F32),
            pltpu.VMEM((ROWS, 128), F32),
            pltpu.VMEM((ROWS, 128), F32),
            dma((2, 2)), dma((4,)), dma((6,)),
        ],
        compiler_params=pltpu.CompilerParams(vmem_limit_bytes=60 * 2**20),
    )(gathered.reshape(32, 2, ROWS, 128), grad, factor, master, momentum)


def solution(mesh):
    fr = ("fsdp", "rep")
    in_specs = (P("rep", "fsdp", None), P("rep", "fsdp"), P(), P(fr, None), P(fr, None))
    out_specs = (P("fsdp", None), P(fr, None), P(fr, None))
    return jax.shard_map(
        per_device, mesh=mesh, in_specs=in_specs, out_specs=out_specs, check_vma=False
    )
```

```python
import functools

import jax
import jax.numpy as jnp
from jax import lax
from jax.experimental import pallas as pl
from jax.experimental.pallas import tpu as pltpu
from jax.sharding import PartitionSpec as P

FF = 28672
MESH = pl.DeviceIdType.MESH
NX, NY, NZ = 4, 2, 8
ROWS = 112
PAD = 128
EARLY = 96
LATE = ROWS - EARLY
AHEAD = 6
SEQUENCE = (
    (0, 4), (0, 3), (0, 5), (1, 4), (0, 2), (0, 6), (1, 3), (1, 5),
    (0, 1), (1, 2), (0, 7), (1, 6), (0, 0), (1, 1), (1, 7), (1, 0),
)
ALONG_ZC = tuple((0, 0, d, c) for c in (1, 0) for d in (4, 3, 5, 2, 6, 1, 7, 0))[:-1]
ALONG_YX = tuple((dx, d, 0, 0) for dx in (2, 1, 3, 0) for d in (4, 3, 5, 2, 6, 1, 7, 0))[:-1]
GREETED = (
    (1, 0, 0, 0), (2, 0, 0, 0), (3, 0, 0, 0), (0, 0, 0, 1), (0, 0, 1, 0), (0, 0, 2, 0), (0, 0, 6, 0), (0, 0, 7, 0),
    (0, 1, 0, 0), (0, 2, 0, 0), (0, 6, 0, 0), (0, 7, 0, 0),
)
BF16, F32 = jnp.bfloat16, jnp.float32


def kernel(
    deltas, scales, clip, master, momentum,
    gathered, grad_out, factor_out,
    scales_v, clip_v, master_v, momentum_v, rx, table, table16, rs, sf, ysrc, yrx, zsrc, zrx, az, gz, nb, cx, nbc, rxl, tl, rl, ylsrc, ylrx, xlsrc, xlrx, sq, ar_rx,
    heard, own_sem, late_sem, in_sem, xs, xr, ss, sr, ys, yr, zs, zr, as_, ar, gs, gr, cs, cr, qs, qr, bs, br, ds_, dr, zls, zlr, tls, tlr, yls, ylr, xls, xlr,
):
    rep, fsdp = lax.axis_index("rep"), lax.axis_index("fsdp")
    x, yl, z = lax.rem(rep, 4), lax.rem(rep // 4, 2), rep // 8
    yh, core = fsdp // 2, lax.rem(fsdp, 2)
    y = yh * 2 + yl

    def device(x, yl, z):
        return ((z * 2 + yl) * 4 + x, fsdp)

    def along_x(d):
        return device(lax.rem(x + d, 4), yl, z)

    def along_z(d):
        return device(x, yl, lax.rem(z + d, 8))

    y_peer = device(x, 1 - yl, z)

    def partner(way):
        dx, dy, dz, dc = way
        to = lax.rem(y + dy, 8)
        return (
            (lax.rem(z + dz, 8) * 2 + lax.rem(to, 2)) * 4 + lax.rem(x + dx, 4),
            (to // 2) * 2 + lax.rem(core + dc, 2),
        )

    barrier = pltpu.get_barrier_semaphore()
    for way in GREETED:
        pl.semaphore_signal(barrier, inc=1, device_id=partner(way), device_id_type=MESH)

    own = pltpu.make_async_copy(deltas.at[:, x, pl.ds(0, EARLY)], rx.at[:, x, pl.ds(0, EARLY)], own_sem)
    own.start()
    late_here = rxl.at[:, :, pl.ds(pl.multiple_of(LATE * z, LATE), LATE)]
    own_late = pltpu.make_async_copy(deltas.at[pl.ds(2 * z, 2), :, pl.ds(EARLY, LATE)], late_here, late_sem)
    own_late.start()
    inputs = [
        pltpu.make_async_copy(here, there, in_sem.at[i])
        for i, (here, there) in enumerate(
            ((scales, scales_v), (master, master_v), (momentum, momentum_v), (clip, clip_v))
        )
    ]
    for copy in inputs:
        copy.start()
    pl.semaphore_wait(barrier, len(GREETED))

    def remote(src, dst, send, recv, to):
        copy = pltpu.make_async_remote_copy(
            src_ref=src, dst_ref=dst, send_sem=send, recv_sem=recv, device_id=to, device_id_type=MESH
        )
        copy.start()
        return copy

    def chunk(mine, dz):
        return 2 * lax.rem(z + dz, 8) + (yl if mine else 1 - yl)

    def send_along_x(s):
        zy = chunk(*SEQUENCE[s])
        return [
            remote(
                deltas.at[zy, lax.rem(x + d, 4), pl.ds(0, EARLY)], rx.at[zy, x, pl.ds(0, EARLY)],
                xs.at[s, k], xr.at[s, k], along_x(d),
            )
            for k, d in enumerate((2, 1, 3))
        ]

    xcopies = [send_along_x(0), send_along_x(1)]
    for d in (1, 2, 6, 7):
        for way in ((0, d, 0, 0), (0, 0, d, 0)):
            pl.semaphore_signal(heard.at[0], inc=1, device_id=partner(way), device_id_type=MESH)
    inputs[0].wait()
    flat = scales_v[...].astype(F32)
    for r in range(NX * NY * NZ):
        table[r % 4, r // 4 : r // 4 + 1, 0:ROWS] = flat[:, ROWS * r : ROWS * (r + 1)]
    for k in range(4):
        table16[k] = table[k].astype(BF16)
    scopies = [
        remote(table16.at[lax.rem(x + d, 4)], rs.at[x], ss.at[k], sr.at[k], along_x(d))
        for k, d in enumerate((2, 1, 3))
    ]
    for s in range(2, AHEAD):
        xcopies.append(send_along_x(s))
    lanes = lax.broadcasted_iota(jnp.int32, (NZ * NY, 128), 1) // LATE == z
    for k in range(4):
        values = jnp.concatenate([table[k][:, EARLY:ROWS]] * 8, axis=1)
        values = jnp.where(lanes, values, 0.0)
        for zy in range(16):
            tl[zy // 2, 4 * (zy % 2) + k : 4 * (zy % 2) + k + 1, :] = values[zy : zy + 1]
    pl.semaphore_wait(heard.at[0], 8)
    lcopies = []
    for i, d in enumerate((4, 3, 5, 2, 6, 1, 7)):
        to = lax.rem(z + d, 8)
        lcopies.append(remote(tl.at[to], rl.at[z], tls.at[i], tlr.at[i], along_z(d)))
        lcopies.append(
            remote(
                deltas.at[pl.ds(2 * to, 2), :, pl.ds(EARLY, LATE)], late_here, zls.at[i], zlr.at[i], along_z(d)
            )
        )

    def spread(blocks, send, recv):
        copies = []
        for i, d in enumerate((1, 7, 2, 6)):
            copies.append(remote(blocks.at[z], blocks.at[z], send.at[i], recv.at[i], along_z(d)))
        return copies

    def pass_on(blocks, send, recv, copies):
        for i, d in ((2, 2), (3, 6)):
            copies[i].wait()
            source = lax.rem(z + 8 - d, 8)
            block = blocks.at[source]
            copies.append(remote(block, block, send.at[i + 2], recv.at[i + 2], along_z(1 if d == 2 else 7)))
            half = blocks.at[source, pl.ds(0 if d == 2 else EARLY // 2, EARLY // 2)]
            copies.append(remote(half, half, send.at[i + 4], recv.at[i + 4], along_z(d)))
        return copies[:2] + copies[4:]

    inputs[1].wait()
    inputs[2].wait()
    moved = master_v[...] - 0.567 * momentum_v[...]
    az[z] = moved[:EARLY]
    cx[yl, x, 0] = moved[EARLY:]

    for zy in range(16):
        for k in range(4):
            rx[zy, k, EARLY:PAD] = jnp.zeros((PAD - EARLY, 128), BF16)
    for copy in scopies:
        copy.wait()
    for k in range(4):
        sf[k] = rs[k].astype(F32)
    sf[x] = table[x]
    own.wait()

    eye = lax.broadcasted_iota(jnp.int32, (EARLY, PAD), 0) == lax.broadcasted_iota(jnp.int32, (EARLY, PAD), 1)

    def decode(zy):
        diags = [
            jnp.where(eye, jnp.broadcast_to(sf[k, pl.ds(zy, 1), :], (EARLY, PAD)), 0.0).astype(BF16)
            for k in range(4)
        ]
        return jnp.dot(
            jnp.concatenate(diags, axis=1), rx[zy].reshape(4 * PAD, 128), preferred_element_type=F32
        )

    late_eye = lax.rem(lax.broadcasted_iota(jnp.int32, (LATE, 128), 1), LATE) == lax.broadcasted_iota(
        jnp.int32, (LATE, 128), 0
    )

    def decode_late(yy, xx, late_scales):
        row = 4 * yy + xx
        diag = jnp.where(late_eye, jnp.broadcast_to(late_scales[pl.ds(row, 1), :], (LATE, 128)), 0.0)
        return jnp.dot(diag.astype(BF16), rxl[yy, xx], preferred_element_type=F32)

    ycopies, zcopies = {}, {}
    for s, (mine, dz) in enumerate(SEQUENCE):
        for copy in xcopies[s]:
            copy.wait()
        if s + AHEAD < len(SEQUENCE):
            xcopies.append(send_along_x(s + AHEAD))
        part = decode(chunk(mine, dz))
        if not mine:
            ysrc[dz] = part
            ycopies[dz] = remote(ysrc.at[dz], yrx.at[dz], ys.at[dz], yr.at[dz], y_peer)
        else:
            ycopies[dz].wait()
            total = part + yrx[dz]
            before = {3: (4,), 2: (3,), 1: (2,), 6: (5,), 7: (6,), 0: (1, 7)}.get(dz, ())
            for far in before:
                zcopies[far].wait()
                total = total + zrx[far - 1]
            if dz:
                zsrc[dz - 1] = total
                zcopies[dz] = remote(
                    zsrc.at[dz - 1], zrx.at[dz - 1], zs.at[dz - 1], zr.at[dz - 1], along_z(1 if dz < 5 else 7)
                )
        if s == 8:
            acopies = spread(az, as_, ar)
        if s == 7:
            for d in (1, 2, 6, 7):
                pl.semaphore_signal(
                    heard.at[1], inc=1, device_id=partner((0, d, 0, 0)), device_id_type=MESH
                )
        if s == 9:
            own_late.wait()
            for copy in lcopies:
                copy.wait()
            rl[z] = tl[z]
            tl[0] = jnp.sum(rl[...], axis=0)
            for xx in range(4):
                ylsrc[xx] = decode_late(1 - yl, xx, tl.at[0])
            ylcopy = remote(ylsrc, ylrx, yls, ylr, y_peer)
            for xx in range(4):
                xlsrc[xx] = decode_late(yl, xx, tl.at[0])
        if s == 12:
            ylcopy.wait()
            for xx in range(4):
                xlsrc[xx] = xlsrc[xx] + ylrx[xx]
            xlcopies = [
                remote(xlsrc.at[lax.rem(x + d, 4)], xlrx.at[k], xls.at[k], xlr.at[k], along_x(d))
                for k, d in enumerate((2, 1, 3))
            ]
    late_total = xlsrc[x]
    for k, copy in enumerate(xlcopies):
        copy.wait()
        late_total = late_total + xlrx[k]
    total = jnp.concatenate([total, late_total], axis=0)
    grad = total * (1.0 / (NX * NY * NZ))
    gz[z] = grad[:EARLY]
    cx[yl, x, 1] = grad[EARLY:]
    pl.semaphore_wait(heard.at[1], 4)
    partial = jnp.sum(grad * grad, axis=0, keepdims=True)
    for stage, ways in enumerate((ALONG_ZC, ALONG_YX)):
        first = stage * len(ALONG_ZC)
        sq[stage] = partial
        copies = [
            remote(sq.at[stage], ar_rx.at[first + i], qs.at[first + i], qr.at[first + i], partner(way))
            for i, way in enumerate(ways)
        ]
        if stage == 0:
            gcopies = spread(gz, gs, gr)
            acopies = pass_on(az, as_, ar, acopies)
            late = [
                remote(
                    cx.at[yl, x], cx.at[yl, x], cs.at[i], cr.at[i],
                    device(lax.rem(x + d, 4), (1 - yl) if other else yl, z),
                )
                for i, (other, d) in enumerate(((1, 2), (1, 1), (1, 3), (1, 0), (0, 2), (0, 1), (0, 3)))
            ]
            grad_out[...] = grad
        else:
            gcopies = pass_on(gz, gs, gr, gcopies)
        for copy in copies:
            copy.wait()
        partial = partial + jnp.sum(ar_rx[first : first + len(ways)], axis=0)
    mean = jnp.sum(partial, axis=1, keepdims=True) * (1.0 / (512 * ROWS * 128))
    inputs[3].wait()
    factor = jnp.minimum(1.0, clip_v[...] / jnp.sqrt(mean + 1e-06))
    factor_out[...] = jnp.broadcast_to(factor, (8, 128))
    step = 1.33 * factor
    for copy in late:
        copy.wait()
    for yy in range(NY):
        for xx in range(NX):
            nbc[yy, xx] = (cx[yy, xx, 0] - step * cx[yy, xx, 1]).astype(BF16)
    here = gathered.at[z, :, :, pl.ds(EARLY, LATE)]
    done = [
        remote(nbc, here, ds_.at[i], dr.at[i], along_z(d)) for i, d in enumerate((4, 3, 5, 2, 6, 1, 7))
    ]
    late_own = pltpu.make_async_copy(nbc, here, late_sem)
    late_own.start()
    for copy in acopies + gcopies:
        copy.wait()

    half = EARLY // 2
    items_a = ((0, 0, EARLY), (1, 0, EARLY), (2, 0, EARLY), (3, 0, half))
    items_b = ((4, 0, EARLY), (5, 0, EARLY), (6, 0, EARLY), (3, half, half), (7, 0, EARLY))
    counter = [0]

    def base_to(item, yy, xx, to, first=False):
        n = counter[0]
        counter[0] += 1
        zi, row, rows = item
        block = gathered.at[zi, yy, xx, pl.ds(row, rows)]
        return remote(nb.at[zi, pl.ds(row, rows)] if first else block, block, bs.at[n], br.at[n], to)

    right, left = along_x(1), along_x(3)
    x_left, x_right = lax.rem(x + 3, 4), lax.rem(x + 1, 4)
    x_far = lax.rem(x + 2, 4)

    def both_ways(item, yy, first=False):
        return base_to(item, yy, x, right, first), base_to(item, yy, x, left, first)

    def further(item, yy, way):
        return base_to(item, yy, x_left, right) if way else base_to(item, yy, x_right, left)

    a_x, b_y = [], []
    for i in range(5):
        for zi in ((0, 4), (1, 5), (2, 6), (3,), (7,))[i]:
            nb[zi] = (az[zi] - step * gz[zi]).astype(BF16)
        b_y.append(base_to(items_b[i], yl, x, y_peer, True))
        if i < 4:
            a_x.append(both_ways(items_a[i], yl, True))
    whole = pltpu.make_async_copy(nb, gathered.at[:, yl, x, pl.ds(0, EARLY)], own_sem)
    whole.start()
    b_x, b_x2, a_far = [], [], []
    for i in range(5):
        if i < 4:
            done.append(base_to(items_a[i], yl, x, y_peer, True))
        b_x.append(both_ways(items_b[i], yl, True))
    for i in range(5):
        if i < 4:
            for copy in a_x[i]:
                copy.wait()
            a_far.append(further(items_a[i], yl, i % 2 == 0))
            done.append(base_to(items_a[i], yl, x_left, y_peer))
            done.append(base_to(items_a[i], yl, x_right, y_peer))
        b_y[i].wait()
        b_x2.append(both_ways(items_b[i], 1 - yl))
    for i in range(5):
        if i < 4:
            a_far[i].wait()
            done.append(base_to(items_a[i], yl, x_far, y_peer))
        for yy, pair, way in ((yl, b_x[i], i % 2 == 1), (1 - yl, b_x2[i], i % 2 == 0)):
            for copy in pair:
                copy.wait()
            done.append(further(items_b[i], yy, way))
    late_own.wait()
    whole.wait()
    for copy in done:
        copy.wait()


def finish_kernel(
    gathered, grad, factor, master, momentum,
    base, new_master, new_momentum,
    rows, master_v, momentum_v, nm_v, nmom_v, small_sem, out_sem,
):
    smalls = [
        pltpu.make_async_copy(here, there, small_sem.at[i])
        for i, (here, there) in enumerate(
            ((master, master_v), (momentum, momentum_v))
        )
    ]
    for copy in smalls:
        copy.start()
    outs = []
    for n in range(4):
        i, h = n // 2, n % 2
        for j in range(0, ROWS, 16):
            turned = jnp.swapaxes(gathered[16 * i : 16 * (i + 1), h, j : j + 16, :], 0, 1)
            for k in range(16):
                rows[i, h, :, 128 * (j + k) : 128 * (j + k + 1)] = turned[k]
        out = pltpu.make_async_copy(
            rows.at[i, h], base.at[pl.ds(16 * i, 16), pl.ds(h * (FF // 2), FF // 2)], out_sem.at[n]
        )
        out.start()
        outs.append(out)
    for copy in smalls:
        copy.wait()
    scaled = factor[0:1, 0:1] * grad[...]
    moved = 0.9 * momentum_v[...] + scaled
    nmom_v[...] = moved
    nm_v[...] = master_v[...] - 0.7 * (scaled + 0.9 * moved)
    outs += [
        pltpu.make_async_copy(nm_v, new_master, out_sem.at[4]),
        pltpu.make_async_copy(nmom_v, new_momentum, out_sem.at[5]),
    ]
    for copy in outs[4:]:
        copy.start()
    for copy in outs:
        copy.wait()


def per_device(deltas, scales, clip_level, master, momentum):
    vmem, anywhere = pl.BlockSpec(memory_space=pltpu.VMEM), pl.BlockSpec(memory_space=pl.ANY)
    dma = pltpu.SemaphoreType.DMA
    deltas, scales, master, momentum = (
        pltpu.with_memory_space_constraint(a, pltpu.HBM)
        for a in (deltas.reshape(NZ * NY, NX, ROWS, 128), scales, master, momentum)
    )
    gathered, grad, factor = pl.pallas_call(
        kernel,
        out_shape=(
            pltpu.VMEM((NZ, NY, NX, ROWS, 128), BF16),
            pltpu.VMEM((ROWS, 128), F32),
            pltpu.VMEM((8, 128), F32),
        ),
        in_specs=[anywhere] * 5,
        out_specs=(vmem, vmem, vmem),
        scratch_shapes=[
            pltpu.VMEM((1, NZ * NY * NX * ROWS), BF16),
            pltpu.VMEM((1, 1), F32),
            pltpu.VMEM((ROWS, 128), F32),
            pltpu.VMEM((ROWS, 128), F32),
            pltpu.VMEM((NZ * NY, NX, PAD, 128), BF16),
            pltpu.VMEM((NX, NZ * NY, 128), F32),
            pltpu.VMEM((NX, NZ * NY, 128), BF16),
            pltpu.VMEM((NX, NZ * NY, 128), BF16),
            pltpu.VMEM((NX, NZ * NY, 128), F32),
            pltpu.VMEM((NZ, EARLY, 128), F32),
            pltpu.VMEM((NZ, EARLY, 128), F32),
            pltpu.VMEM((NZ - 1, EARLY, 128), F32),
            pltpu.VMEM((NZ - 1, EARLY, 128), F32),
            pltpu.VMEM((NZ, EARLY, 128), F32),
            pltpu.VMEM((NZ, EARLY, 128), F32),
            pltpu.VMEM((NZ, EARLY, 128), BF16),
            pltpu.VMEM((NY, NX, 2, LATE, 128), F32),
            pltpu.VMEM((NY, NX, LATE, 128), BF16),
            pltpu.VMEM((NY, NX, NZ * LATE, 128), BF16),
            pltpu.VMEM((NZ, NY * NX, 128), F32),
            pltpu.VMEM((NZ, NY * NX, 128), F32),
            pltpu.VMEM((NX, LATE, 128), F32),
            pltpu.VMEM((NX, LATE, 128), F32),
            pltpu.VMEM((NX, LATE, 128), F32),
            pltpu.VMEM((NX - 1, LATE, 128), F32),
            pltpu.VMEM((2, 1, 128), F32),
            pltpu.VMEM((46, 1, 128), F32),
            pltpu.SemaphoreType.REGULAR((2,)),
            dma,
            dma,
            dma((4,)),
            dma((16, 3)), dma((16, 3)),
            dma((3,)), dma((3,)),
            dma((8,)), dma((8,)),
            dma((7,)), dma((7,)),
            dma((8,)), dma((8,)),
            dma((8,)), dma((8,)),
            dma((7,)), dma((7,)),
            dma((46,)), dma((46,)),
            dma((63,)), dma((63,)),
            dma((7,)), dma((7,)),
            dma((7,)), dma((7,)),
            dma((7,)), dma((7,)),
            dma, dma,
            dma((3,)), dma((3,)),
        ],
        compiler_params=pltpu.CompilerParams(
            collective_id=0, has_side_effects=True, vmem_limit_bytes=40 * 2**20
        ),
    )(
        deltas, scales, clip_level.reshape(1, 1), master, momentum
    )
    half = FF // 2
    return pl.pallas_call(
        finish_kernel,
        out_shape=(
            jax.ShapeDtypeStruct((32, FF), BF16),
            jax.ShapeDtypeStruct((ROWS, 128), F32),
            jax.ShapeDtypeStruct((ROWS, 128), F32),
        ),
        in_specs=[vmem] * 3 + [anywhere] * 2,
        out_specs=(anywhere,) * 3,
        scratch_shapes=[
            pltpu.VMEM((2, 2, 16, half), BF16),
            pltpu.VMEM((ROWS, 128), F32),
            pltpu.VMEM((ROWS, 128), F32),
            pltpu.VMEM((ROWS, 128), F32),
            pltpu.VMEM((ROWS, 128), F32),
            dma((2,)), dma((6,)),
        ],
        compiler_params=pltpu.CompilerParams(vmem_limit_bytes=40 * 2**20),
    )(gathered.reshape(32, 2, ROWS, 128), grad, factor, master, momentum)


def solution(mesh):
    fr = ("fsdp", "rep")
    in_specs = (P("rep", "fsdp", None), P("rep", "fsdp"), P(), P(fr, None), P(fr, None))
    out_specs = (P("fsdp", None), P(fr, None), P(fr, None))
    return jax.shard_map(
        per_device, mesh=mesh, in_specs=in_specs, out_specs=out_specs, check_vma=False
    )
```

```python
import functools

import jax
import jax.numpy as jnp
from jax import lax
from jax.experimental import pallas as pl
from jax.experimental.pallas import tpu as pltpu
from jax.sharding import PartitionSpec as P

FF = 28672
MESH = pl.DeviceIdType.MESH
NX, NY, NZ = 4, 2, 8
ROWS = 112
PAD = 128
EARLY = 96
LATE = ROWS - EARLY
FIRST, HALF = 88, 48
LAST = ROWS - FIRST
AHEAD = 6
SEQUENCE = (
    (0, 4), (0, 3), (0, 5), (1, 4), (0, 2), (1, 3), (0, 6), (1, 5),
    (0, 1), (1, 2), (0, 7), (1, 6), (1, 1), (0, 0), (1, 7), (1, 0),
)
ALONG_ZC = tuple((0, 0, d, c) for c in (1, 0) for d in (4, 3, 5, 2, 6, 1, 7, 0))[:-1]
ALONG_YX = tuple((dx, d, 0, 0) for dx in (2, 1, 3, 0) for d in (4, 3, 5, 2, 6, 1, 7, 0))[:-1]
GREETED = (
    (1, 0, 0, 0), (2, 0, 0, 0), (3, 0, 0, 0), (0, 0, 0, 1), (0, 0, 1, 0), (0, 0, 2, 0), (0, 0, 6, 0), (0, 0, 7, 0),
    (0, 1, 0, 0), (0, 2, 0, 0), (0, 6, 0, 0), (0, 7, 0, 0),
)
BF16, F32 = jnp.bfloat16, jnp.float32


def kernel(
    deltas, scales, clip, master, momentum,
    gathered, grad_out, factor_out,
    scales_v, clip_v, master_v, momentum_v, rx, table, table16, rs, sf, ysrc, yrx, zsrc, zrx, az, gz, nb, cx, nbc, rxl, tl, rl, ylsrc, ylrx, xlsrc, xlrx, sq, ar_rx,
    heard, own_sem, late_sem, in_sem, xs, xr, ss, sr, ys, yr, zs, zr, as_, ar, gs, gr, cs, cr, qs, qr, bs, br, ds_, dr, zls, zlr, tls, tlr, yls, ylr, xls, xlr,
):
    rep, fsdp = lax.axis_index("rep"), lax.axis_index("fsdp")
    x, yl, z = lax.rem(rep, 4), lax.rem(rep // 4, 2), rep // 8
    yh, core = fsdp // 2, lax.rem(fsdp, 2)
    y = yh * 2 + yl

    def device(x, yl, z):
        return ((z * 2 + yl) * 4 + x, fsdp)

    def along_x(d):
        return device(lax.rem(x + d, 4), yl, z)

    def along_z(d):
        return device(x, yl, lax.rem(z + d, 8))

    y_peer = device(x, 1 - yl, z)

    def partner(way):
        dx, dy, dz, dc = way
        to = lax.rem(y + dy, 8)
        return (
            (lax.rem(z + dz, 8) * 2 + lax.rem(to, 2)) * 4 + lax.rem(x + dx, 4),
            (to // 2) * 2 + lax.rem(core + dc, 2),
        )

    barrier = pltpu.get_barrier_semaphore()
    for way in GREETED:
        pl.semaphore_signal(barrier, inc=1, device_id=partner(way), device_id_type=MESH)

    own = pltpu.make_async_copy(deltas.at[:, x, pl.ds(0, EARLY)], rx.at[:, x, pl.ds(0, EARLY)], own_sem)
    own.start()
    late_here = rxl.at[:, :, pl.ds(pl.multiple_of(LATE * z, LATE), LATE)]
    own_late = pltpu.make_async_copy(deltas.at[pl.ds(2 * z, 2), :, pl.ds(EARLY, LATE)], late_here, late_sem)
    own_late.start()
    inputs = [
        pltpu.make_async_copy(here, there, in_sem.at[i])
        for i, (here, there) in enumerate(
            ((scales, scales_v), (master, master_v), (momentum, momentum_v), (clip, clip_v))
        )
    ]
    for copy in inputs:
        copy.start()
    pl.semaphore_wait(barrier, len(GREETED))

    def remote(src, dst, send, recv, to):
        copy = pltpu.make_async_remote_copy(
            src_ref=src, dst_ref=dst, send_sem=send, recv_sem=recv, device_id=to, device_id_type=MESH
        )
        copy.start()
        return copy

    def chunk(mine, dz):
        return 2 * lax.rem(z + dz, 8) + (yl if mine else 1 - yl)

    def send_along_x(s):
        zy = chunk(*SEQUENCE[s])
        return [
            remote(
                deltas.at[zy, lax.rem(x + d, 4), pl.ds(0, EARLY)], rx.at[zy, x, pl.ds(0, EARLY)],
                xs.at[s, k], xr.at[s, k], along_x(d),
            )
            for k, d in enumerate((2, 1, 3))
        ]

    xcopies = [send_along_x(0), send_along_x(1)]
    for d in (1, 2, 6, 7):
        for way in ((0, d, 0, 0), (0, 0, d, 0)):
            pl.semaphore_signal(heard.at[0], inc=1, device_id=partner(way), device_id_type=MESH)
    inputs[0].wait()
    flat = scales_v[...].astype(F32)
    for r in range(NX * NY * NZ):
        table[r % 4, r // 4 : r // 4 + 1, 0:ROWS] = flat[:, ROWS * r : ROWS * (r + 1)]
    for k in range(4):
        table16[k] = table[k].astype(BF16)
    scopies = [
        remote(table16.at[lax.rem(x + d, 4)], rs.at[x], ss.at[k], sr.at[k], along_x(d))
        for k, d in enumerate((2, 1, 3))
    ]
    for s in range(2, AHEAD):
        xcopies.append(send_along_x(s))
    lanes = lax.broadcasted_iota(jnp.int32, (NZ * NY, 128), 1) // LATE == z
    for k in range(4):
        values = jnp.concatenate([table[k][:, EARLY:ROWS]] * 8, axis=1)
        values = jnp.where(lanes, values, 0.0)
        for zy in range(16):
            tl[zy // 2, 4 * (zy % 2) + k : 4 * (zy % 2) + k + 1, :] = values[zy : zy + 1]
    pl.semaphore_wait(heard.at[0], 8)
    lcopies = []
    for i, d in enumerate((4, 3, 5, 2, 6, 1, 7)):
        to = lax.rem(z + d, 8)
        lcopies.append(remote(tl.at[to], rl.at[z], tls.at[i], tlr.at[i], along_z(d)))
        lcopies.append(
            remote(
                deltas.at[pl.ds(2 * to, 2), :, pl.ds(EARLY, LATE)], late_here, zls.at[i], zlr.at[i], along_z(d)
            )
        )

    def spread(blocks, send, recv):
        copies = []
        for i, d in enumerate((1, 7, 2, 6)):
            copies.append(remote(blocks.at[z], blocks.at[z], send.at[i], recv.at[i], along_z(d)))
        return copies

    def pass_on(blocks, send, recv, copies):
        for i, d in ((2, 2), (3, 6)):
            copies[i].wait()
            source = lax.rem(z + 8 - d, 8)
            block = blocks.at[source]
            copies.append(remote(block, block, send.at[i + 2], recv.at[i + 2], along_z(1 if d == 2 else 7)))
            half = blocks.at[source, pl.ds(0, HALF) if d == 2 else pl.ds(HALF, FIRST - HALF)]
            copies.append(remote(half, half, send.at[i + 4], recv.at[i + 4], along_z(d)))
        return copies[:2] + copies[4:]

    inputs[1].wait()
    inputs[2].wait()
    moved = master_v[...] - 0.567 * momentum_v[...]
    az[z] = moved[:FIRST]
    cx[yl, x, 0] = moved[FIRST:]

    for zy in range(16):
        for k in range(4):
            rx[zy, k, EARLY:PAD] = jnp.zeros((PAD - EARLY, 128), BF16)
    for copy in scopies:
        copy.wait()
    for k in range(4):
        sf[k] = rs[k].astype(F32)
    sf[x] = table[x]
    own.wait()

    eye = lax.broadcasted_iota(jnp.int32, (EARLY, PAD), 0) == lax.broadcasted_iota(jnp.int32, (EARLY, PAD), 1)

    def decode(zy):
        diags = [
            jnp.where(eye, jnp.broadcast_to(sf[k, pl.ds(zy, 1), :], (EARLY, PAD)), 0.0).astype(BF16)
            for k in range(4)
        ]
        return jnp.dot(
            jnp.concatenate(diags, axis=1), rx[zy].reshape(4 * PAD, 128), preferred_element_type=F32
        )

    late_eye = lax.rem(lax.broadcasted_iota(jnp.int32, (LATE, 128), 1), LATE) == lax.broadcasted_iota(
        jnp.int32, (LATE, 128), 0
    )

    def decode_late(yy, xx, late_scales):
        row = 4 * yy + xx
        diag = jnp.where(late_eye, jnp.broadcast_to(late_scales[pl.ds(row, 1), :], (LATE, 128)), 0.0)
        return jnp.dot(diag.astype(BF16), rxl[yy, xx], preferred_element_type=F32)

    ycopies, zcopies = {}, {}
    for s, (mine, dz) in enumerate(SEQUENCE):
        for copy in xcopies[s]:
            copy.wait()
        if s + AHEAD < len(SEQUENCE):
            xcopies.append(send_along_x(s + AHEAD))
        part = decode(chunk(mine, dz))
        if not mine:
            ysrc[dz] = part
            ycopies[dz] = remote(ysrc.at[dz], yrx.at[dz], ys.at[dz], yr.at[dz], y_peer)
        else:
            ycopies[dz].wait()
            total = part + yrx[dz]
            before = {3: (4,), 2: (3,), 1: (2,), 6: (5,), 7: (6,), 0: (1, 7)}.get(dz, ())
            for far in before:
                zcopies[far].wait()
                total = total + zrx[far - 1]
            if dz:
                zsrc[dz - 1] = total
                zcopies[dz] = remote(
                    zsrc.at[dz - 1], zrx.at[dz - 1], zs.at[dz - 1], zr.at[dz - 1], along_z(1 if dz < 5 else 7)
                )
        if s == 8:
            acopies = spread(az, as_, ar)
        if s == 7:
            for d in (1, 2, 6, 7):
                pl.semaphore_signal(
                    heard.at[1], inc=1, device_id=partner((0, d, 0, 0)), device_id_type=MESH
                )
        if s == 9:
            own_late.wait()
            for copy in lcopies:
                copy.wait()
            rl[z] = tl[z]
            tl[0] = jnp.sum(rl[...], axis=0)
            for xx in range(4):
                ylsrc[xx] = decode_late(1 - yl, xx, tl.at[0])
            ylcopy = remote(ylsrc, ylrx, yls, ylr, y_peer)
            for xx in range(4):
                xlsrc[xx] = decode_late(yl, xx, tl.at[0])
        if s == 12:
            ylcopy.wait()
            for xx in range(4):
                xlsrc[xx] = xlsrc[xx] + ylrx[xx]
            xlcopies = [
                remote(xlsrc.at[lax.rem(x + d, 4)], xlrx.at[k], xls.at[k], xlr.at[k], along_x(d))
                for k, d in enumerate((2, 1, 3))
            ]
    late_total = xlsrc[x]
    for k, copy in enumerate(xlcopies):
        copy.wait()
        late_total = late_total + xlrx[k]
    total = jnp.concatenate([total, late_total], axis=0)
    grad = total * (1.0 / (NX * NY * NZ))
    gz[z] = grad[:FIRST]
    cx[yl, x, 1] = grad[FIRST:]
    pl.semaphore_wait(heard.at[1], 4)
    partial = jnp.sum(grad * grad, axis=0, keepdims=True)
    for stage, ways in enumerate((ALONG_ZC, ALONG_YX)):
        first = stage * len(ALONG_ZC)
        sq[stage] = partial
        copies = [
            remote(sq.at[stage], ar_rx.at[first + i], qs.at[first + i], qr.at[first + i], partner(way))
            for i, way in enumerate(ways)
        ]
        if stage == 0:
            gcopies = spread(gz, gs, gr)
            acopies = pass_on(az, as_, ar, acopies)
            late = [
                remote(
                    cx.at[yl, x], cx.at[yl, x], cs.at[i], cr.at[i],
                    device(lax.rem(x + d, 4), (1 - yl) if other else yl, z),
                )
                for i, (other, d) in enumerate(((1, 2), (1, 1), (1, 3), (1, 0), (0, 2), (0, 1), (0, 3)))
            ]
            grad_out[...] = grad
        else:
            gcopies = pass_on(gz, gs, gr, gcopies)
        for copy in copies:
            copy.wait()
        partial = partial + jnp.sum(ar_rx[first : first + len(ways)], axis=0)
    mean = jnp.sum(partial, axis=1, keepdims=True) * (1.0 / (512 * ROWS * 128))
    inputs[3].wait()
    factor = jnp.minimum(1.0, clip_v[...] / jnp.sqrt(mean + 1e-06))
    factor_out[...] = jnp.broadcast_to(factor, (8, 128))
    step = 1.33 * factor
    for copy in late:
        copy.wait()
    for yy in range(NY):
        for xx in range(NX):
            nbc[yy, xx] = (cx[yy, xx, 0] - step * cx[yy, xx, 1]).astype(BF16)
    here = gathered.at[z, :, :, pl.ds(FIRST, LAST)]
    done = [
        remote(nbc, here, ds_.at[i], dr.at[i], along_z(d)) for i, d in enumerate((4, 3, 5, 2, 6, 1, 7))
    ]
    late_own = pltpu.make_async_copy(nbc, here, late_sem)
    late_own.start()
    for copy in acopies + gcopies:
        copy.wait()

    items_a = ((0, 0, FIRST), (1, 0, FIRST), (2, 0, FIRST), (3, 0, HALF))
    items_b = ((4, 0, FIRST), (5, 0, FIRST), (6, 0, FIRST), (3, HALF, FIRST - HALF), (7, 0, FIRST))
    counter = [0]

    def base_to(item, yy, xx, to, first=False):
        n = counter[0]
        counter[0] += 1
        zi, row, rows = item
        block = gathered.at[zi, yy, xx, pl.ds(row, rows)]
        return remote(nb.at[zi, pl.ds(row, rows)] if first else block, block, bs.at[n], br.at[n], to)

    right, left = along_x(1), along_x(3)
    x_left, x_right = lax.rem(x + 3, 4), lax.rem(x + 1, 4)
    x_far = lax.rem(x + 2, 4)

    def both_ways(item, yy, first=False):
        return base_to(item, yy, x, right, first), base_to(item, yy, x, left, first)

    def further(item, yy, way):
        return base_to(item, yy, x_left, right) if way else base_to(item, yy, x_right, left)

    a_x, b_y = [], []
    for i in range(5):
        for zi in ((0, 4), (1, 5), (2, 6), (3,), (7,))[i]:
            nb[zi] = (az[zi] - step * gz[zi]).astype(BF16)
        b_y.append(base_to(items_b[i], yl, x, y_peer, True))
        if i < 4:
            a_x.append(both_ways(items_a[i], yl, True))
    whole = pltpu.make_async_copy(nb, gathered.at[:, yl, x, pl.ds(0, FIRST)], own_sem)
    whole.start()
    b_x, b_x2, a_far = [], [], []
    for i in range(5):
        if i < 4:
            done.append(base_to(items_a[i], yl, x, y_peer, True))
        b_x.append(both_ways(items_b[i], yl, True))
    for i in range(5):
        if i < 4:
            for copy in a_x[i]:
                copy.wait()
            a_far.append(further(items_a[i], yl, i % 2 == 0))
            done.append(base_to(items_a[i], yl, x_left, y_peer))
            done.append(base_to(items_a[i], yl, x_right, y_peer))
        b_y[i].wait()
        b_x2.append(both_ways(items_b[i], 1 - yl))
    for i in range(5):
        if i < 4:
            a_far[i].wait()
            done.append(base_to(items_a[i], yl, x_far, y_peer))
        for yy, pair, way in ((yl, b_x[i], i % 2 == 1), (1 - yl, b_x2[i], i % 2 == 0)):
            for copy in pair:
                copy.wait()
            done.append(further(items_b[i], yy, way))
    late_own.wait()
    whole.wait()
    for copy in done:
        copy.wait()


def finish_kernel(
    gathered, grad, factor, master, momentum,
    base, new_master, new_momentum,
    rows, master_v, momentum_v, nm_v, nmom_v, small_sem, out_sem,
):
    smalls = [
        pltpu.make_async_copy(here, there, small_sem.at[i])
        for i, (here, there) in enumerate(
            ((master, master_v), (momentum, momentum_v))
        )
    ]
    for copy in smalls:
        copy.start()
    outs = []
    for n in range(4):
        i, h = n // 2, n % 2
        for j in range(0, ROWS, 16):
            turned = jnp.swapaxes(gathered[16 * i : 16 * (i + 1), h, j : j + 16, :], 0, 1)
            for k in range(16):
                rows[i, h, :, 128 * (j + k) : 128 * (j + k + 1)] = turned[k]
        out = pltpu.make_async_copy(
            rows.at[i, h], base.at[pl.ds(16 * i, 16), pl.ds(h * (FF // 2), FF // 2)], out_sem.at[n]
        )
        out.start()
        outs.append(out)
    for copy in smalls:
        copy.wait()
    scaled = factor[0:1, 0:1] * grad[...]
    moved = 0.9 * momentum_v[...] + scaled
    nmom_v[...] = moved
    nm_v[...] = master_v[...] - 0.7 * (scaled + 0.9 * moved)
    outs += [
        pltpu.make_async_copy(nm_v, new_master, out_sem.at[4]),
        pltpu.make_async_copy(nmom_v, new_momentum, out_sem.at[5]),
    ]
    for copy in outs[4:]:
        copy.start()
    for copy in outs:
        copy.wait()


def per_device(deltas, scales, clip_level, master, momentum):
    vmem, anywhere = pl.BlockSpec(memory_space=pltpu.VMEM), pl.BlockSpec(memory_space=pl.ANY)
    dma = pltpu.SemaphoreType.DMA
    deltas, scales, master, momentum = (
        pltpu.with_memory_space_constraint(a, pltpu.HBM)
        for a in (deltas.reshape(NZ * NY, NX, ROWS, 128), scales, master, momentum)
    )
    gathered, grad, factor = pl.pallas_call(
        kernel,
        out_shape=(
            pltpu.VMEM((NZ, NY, NX, ROWS, 128), BF16),
            pltpu.VMEM((ROWS, 128), F32),
            pltpu.VMEM((8, 128), F32),
        ),
        in_specs=[anywhere] * 5,
        out_specs=(vmem, vmem, vmem),
        scratch_shapes=[
            pltpu.VMEM((1, NZ * NY * NX * ROWS), BF16),
            pltpu.VMEM((1, 1), F32),
            pltpu.VMEM((ROWS, 128), F32),
            pltpu.VMEM((ROWS, 128), F32),
            pltpu.VMEM((NZ * NY, NX, PAD, 128), BF16),
            pltpu.VMEM((NX, NZ * NY, 128), F32),
            pltpu.VMEM((NX, NZ * NY, 128), BF16),
            pltpu.VMEM((NX, NZ * NY, 128), BF16),
            pltpu.VMEM((NX, NZ * NY, 128), F32),
            pltpu.VMEM((NZ, EARLY, 128), F32),
            pltpu.VMEM((NZ, EARLY, 128), F32),
            pltpu.VMEM((NZ - 1, EARLY, 128), F32),
            pltpu.VMEM((NZ - 1, EARLY, 128), F32),
            pltpu.VMEM((NZ, FIRST, 128), F32),
            pltpu.VMEM((NZ, FIRST, 128), F32),
            pltpu.VMEM((NZ, FIRST, 128), BF16),
            pltpu.VMEM((NY, NX, 2, LAST, 128), F32),
            pltpu.VMEM((NY, NX, LAST, 128), BF16),
            pltpu.VMEM((NY, NX, NZ * LATE, 128), BF16),
            pltpu.VMEM((NZ, NY * NX, 128), F32),
            pltpu.VMEM((NZ, NY * NX, 128), F32),
            pltpu.VMEM((NX, LATE, 128), F32),
            pltpu.VMEM((NX, LATE, 128), F32),
            pltpu.VMEM((NX, LATE, 128), F32),
            pltpu.VMEM((NX - 1, LATE, 128), F32),
            pltpu.VMEM((2, 1, 128), F32),
            pltpu.VMEM((46, 1, 128), F32),
            pltpu.SemaphoreType.REGULAR((2,)),
            dma,
            dma,
            dma((4,)),
            dma((16, 3)), dma((16, 3)),
            dma((3,)), dma((3,)),
            dma((8,)), dma((8,)),
            dma((7,)), dma((7,)),
            dma((8,)), dma((8,)),
            dma((8,)), dma((8,)),
            dma((7,)), dma((7,)),
            dma((46,)), dma((46,)),
            dma((63,)), dma((63,)),
            dma((7,)), dma((7,)),
            dma((7,)), dma((7,)),
            dma((7,)), dma((7,)),
            dma, dma,
            dma((3,)), dma((3,)),
        ],
        compiler_params=pltpu.CompilerParams(
            collective_id=0, has_side_effects=True, vmem_limit_bytes=40 * 2**20
        ),
    )(
        deltas, scales, clip_level.reshape(1, 1), master, momentum
    )
    half = FF // 2
    return pl.pallas_call(
        finish_kernel,
        out_shape=(
            jax.ShapeDtypeStruct((32, FF), BF16),
            jax.ShapeDtypeStruct((ROWS, 128), F32),
            jax.ShapeDtypeStruct((ROWS, 128), F32),
        ),
        in_specs=[vmem] * 3 + [anywhere] * 2,
        out_specs=(anywhere,) * 3,
        scratch_shapes=[
            pltpu.VMEM((2, 2, 16, half), BF16),
            pltpu.VMEM((ROWS, 128), F32),
            pltpu.VMEM((ROWS, 128), F32),
            pltpu.VMEM((ROWS, 128), F32),
            pltpu.VMEM((ROWS, 128), F32),
            dma((2,)), dma((6,)),
        ],
        compiler_params=pltpu.CompilerParams(vmem_limit_bytes=40 * 2**20),
    )(gathered.reshape(32, 2, ROWS, 128), grad, factor, master, momentum)


def solution(mesh):
    fr = ("fsdp", "rep")
    in_specs = (P("rep", "fsdp", None), P("rep", "fsdp"), P(), P(fr, None), P(fr, None))
    out_specs = (P("fsdp", None), P(fr, None), P(fr, None))
    return jax.shard_map(
        per_device, mesh=mesh, in_specs=in_specs, out_specs=out_specs, check_vma=False
    )
```

```python
import functools

import jax
import jax.numpy as jnp
from jax import lax
from jax.experimental import pallas as pl
from jax.experimental.pallas import tpu as pltpu
from jax.sharding import PartitionSpec as P

FF = 28672
MESH = pl.DeviceIdType.MESH
NX, NY, NZ = 4, 2, 8
ROWS = 112
PAD = 128
EARLY = 96
LATE = ROWS - EARLY
FIRST, HALF = 88, 48
LAST = ROWS - FIRST
AHEAD = 8
SEQUENCE = (
    (0, 4), (0, 3), (0, 5), (1, 4), (0, 2), (1, 3), (0, 6), (1, 5),
    (0, 1), (1, 2), (0, 7), (1, 6), (1, 1), (0, 0), (1, 7), (1, 0),
)
ALONG_ZC = tuple((0, 0, d, c) for c in (1, 0) for d in (4, 3, 5, 2, 6, 1, 7, 0))[:-1]
ALONG_YX = tuple((dx, d, 0, 0) for dx in (2, 1, 3, 0) for d in (4, 3, 5, 2, 6, 1, 7, 0))[:-1]
GREETED = (
    (1, 0, 0, 0), (2, 0, 0, 0), (3, 0, 0, 0), (0, 0, 0, 1), (0, 0, 1, 0), (0, 0, 2, 0), (0, 0, 6, 0), (0, 0, 7, 0),
    (0, 1, 0, 0), (0, 2, 0, 0), (0, 6, 0, 0), (0, 7, 0, 0),
)
BF16, F32 = jnp.bfloat16, jnp.float32


def kernel(
    deltas, scales, clip, master, momentum,
    gathered, grad_out, factor_out,
    scales_v, clip_v, master_v, momentum_v, rx, table, table16, rs, sf, ysrc, yrx, zsrc, zrx, az, gz, nb, cx, nbc, rxl, tl, rl, ylsrc, ylrx, xlsrc, xlrx, sq, ar_rx,
    heard, own_sem, late_sem, in_sem, xs, xr, ss, sr, ys, yr, zs, zr, as_, ar, gs, gr, cs, cr, qs, qr, bs, br, ds_, dr, zls, zlr, tls, tlr, yls, ylr, xls, xlr,
):
    rep, fsdp = lax.axis_index("rep"), lax.axis_index("fsdp")
    x, yl, z = lax.rem(rep, 4), lax.rem(rep // 4, 2), rep // 8
    yh, core = fsdp // 2, lax.rem(fsdp, 2)
    y = yh * 2 + yl

    def device(x, yl, z):
        return ((z * 2 + yl) * 4 + x, fsdp)

    def along_x(d):
        return device(lax.rem(x + d, 4), yl, z)

    def along_z(d):
        return device(x, yl, lax.rem(z + d, 8))

    y_peer = device(x, 1 - yl, z)

    def partner(way):
        dx, dy, dz, dc = way
        to = lax.rem(y + dy, 8)
        return (
            (lax.rem(z + dz, 8) * 2 + lax.rem(to, 2)) * 4 + lax.rem(x + dx, 4),
            (to // 2) * 2 + lax.rem(core + dc, 2),
        )

    barrier = pltpu.get_barrier_semaphore()
    for way in GREETED:
        pl.semaphore_signal(barrier, inc=1, device_id=partner(way), device_id_type=MESH)

    own = pltpu.make_async_copy(deltas.at[:, x, pl.ds(0, EARLY)], rx.at[:, x, pl.ds(0, EARLY)], own_sem)
    own.start()
    late_here = rxl.at[:, :, pl.ds(pl.multiple_of(LATE * z, LATE), LATE)]
    own_late = pltpu.make_async_copy(deltas.at[pl.ds(2 * z, 2), :, pl.ds(EARLY, LATE)], late_here, late_sem)
    own_late.start()
    inputs = [
        pltpu.make_async_copy(here, there, in_sem.at[i])
        for i, (here, there) in enumerate(
            ((scales, scales_v), (master, master_v), (momentum, momentum_v), (clip, clip_v))
        )
    ]
    for copy in inputs:
        copy.start()
    pl.semaphore_wait(barrier, len(GREETED))

    def remote(src, dst, send, recv, to):
        copy = pltpu.make_async_remote_copy(
            src_ref=src, dst_ref=dst, send_sem=send, recv_sem=recv, device_id=to, device_id_type=MESH
        )
        copy.start()
        return copy

    def chunk(mine, dz):
        return 2 * lax.rem(z + dz, 8) + (yl if mine else 1 - yl)

    def send_along_x(s):
        zy = chunk(*SEQUENCE[s])
        return [
            remote(
                deltas.at[zy, lax.rem(x + d, 4), pl.ds(0, EARLY)], rx.at[zy, x, pl.ds(0, EARLY)],
                xs.at[s, k], xr.at[s, k], along_x(d),
            )
            for k, d in enumerate((2, 1, 3))
        ]

    xcopies = [send_along_x(s) for s in range(3)]
    for d in (1, 2, 6, 7):
        for way in ((0, d, 0, 0), (0, 0, d, 0)):
            pl.semaphore_signal(heard.at[0], inc=1, device_id=partner(way), device_id_type=MESH)
    inputs[0].wait()
    flat = scales_v[...].astype(F32)
    for r in range(NX * NY * NZ):
        table[r % 4, r // 4 : r // 4 + 1, 0:ROWS] = flat[:, ROWS * r : ROWS * (r + 1)]
    for k in range(4):
        table16[k] = table[k].astype(BF16)
    scopies = [
        remote(table16.at[lax.rem(x + d, 4)], rs.at[x], ss.at[k], sr.at[k], along_x(d))
        for k, d in enumerate((2, 1, 3))
    ]
    for s in range(3, AHEAD):
        xcopies.append(send_along_x(s))
    lanes = lax.broadcasted_iota(jnp.int32, (NZ * NY, 128), 1) // LATE == z
    for k in range(4):
        values = jnp.concatenate([table[k][:, EARLY:ROWS]] * 8, axis=1)
        values = jnp.where(lanes, values, 0.0)
        for zy in range(16):
            tl[zy // 2, 4 * (zy % 2) + k : 4 * (zy % 2) + k + 1, :] = values[zy : zy + 1]
    pl.semaphore_wait(heard.at[0], 8)
    lcopies = []
    for i, d in enumerate((4, 3, 5, 2, 6, 1, 7)):
        to = lax.rem(z + d, 8)
        lcopies.append(remote(tl.at[to], rl.at[z], tls.at[i], tlr.at[i], along_z(d)))
        lcopies.append(
            remote(
                deltas.at[pl.ds(2 * to, 2), :, pl.ds(EARLY, LATE)], late_here, zls.at[i], zlr.at[i], along_z(d)
            )
        )

    def spread(blocks, send, recv):
        copies = []
        for i, d in enumerate((1, 7, 2, 6)):
            copies.append(remote(blocks.at[z], blocks.at[z], send.at[i], recv.at[i], along_z(d)))
        return copies

    def pass_on(blocks, send, recv, copies):
        for i, d in ((2, 2), (3, 6)):
            copies[i].wait()
            source = lax.rem(z + 8 - d, 8)
            block = blocks.at[source]
            copies.append(remote(block, block, send.at[i + 2], recv.at[i + 2], along_z(1 if d == 2 else 7)))
            half = blocks.at[source, pl.ds(0, HALF) if d == 2 else pl.ds(HALF, FIRST - HALF)]
            copies.append(remote(half, half, send.at[i + 4], recv.at[i + 4], along_z(d)))
        return copies[:2] + copies[4:]

    inputs[1].wait()
    inputs[2].wait()
    moved = master_v[...] - 0.567 * momentum_v[...]
    az[z] = moved[:FIRST]
    cx[yl, x, 0] = moved[FIRST:]

    for zy in range(16):
        for k in range(4):
            rx[zy, k, EARLY:PAD] = jnp.zeros((PAD - EARLY, 128), BF16)
    for copy in scopies:
        copy.wait()
    for k in range(4):
        sf[k] = rs[k].astype(F32)
    sf[x] = table[x]
    own.wait()

    eye = lax.broadcasted_iota(jnp.int32, (EARLY, PAD), 0) == lax.broadcasted_iota(jnp.int32, (EARLY, PAD), 1)

    def decode(zy):
        diags = [
            jnp.where(eye, jnp.broadcast_to(sf[k, pl.ds(zy, 1), :], (EARLY, PAD)), 0.0).astype(BF16)
            for k in range(4)
        ]
        return jnp.dot(
            jnp.concatenate(diags, axis=1), rx[zy].reshape(4 * PAD, 128), preferred_element_type=F32
        )

    late_eye = lax.rem(lax.broadcasted_iota(jnp.int32, (LATE, 128), 1), LATE) == lax.broadcasted_iota(
        jnp.int32, (LATE, 128), 0
    )

    def decode_late(yy, xx, late_scales):
        row = 4 * yy + xx
        diag = jnp.where(late_eye, jnp.broadcast_to(late_scales[pl.ds(row, 1), :], (LATE, 128)), 0.0)
        return jnp.dot(diag.astype(BF16), rxl[yy, xx], preferred_element_type=F32)

    ycopies, zcopies = {}, {}
    for s, (mine, dz) in enumerate(SEQUENCE):
        for copy in xcopies[s]:
            copy.wait()
        if s + AHEAD < len(SEQUENCE):
            xcopies.append(send_along_x(s + AHEAD))
        part = decode(chunk(mine, dz))
        if not mine:
            ysrc[dz] = part
            ycopies[dz] = remote(ysrc.at[dz], yrx.at[dz], ys.at[dz], yr.at[dz], y_peer)
        else:
            ycopies[dz].wait()
            total = part + yrx[dz]
            before = {3: (4,), 2: (3,), 1: (2,), 6: (5,), 7: (6,), 0: (1, 7)}.get(dz, ())
            for far in before:
                zcopies[far].wait()
                total = total + zrx[far - 1]
            if dz:
                zsrc[dz - 1] = total
                zcopies[dz] = remote(
                    zsrc.at[dz - 1], zrx.at[dz - 1], zs.at[dz - 1], zr.at[dz - 1], along_z(1 if dz < 5 else 7)
                )
        if s == 8:
            acopies = spread(az, as_, ar)
        if s == 7:
            for d in (1, 2, 6, 7):
                pl.semaphore_signal(
                    heard.at[1], inc=1, device_id=partner((0, d, 0, 0)), device_id_type=MESH
                )
        if s == 9:
            own_late.wait()
            for copy in lcopies:
                copy.wait()
            rl[z] = tl[z]
            tl[0] = jnp.sum(rl[...], axis=0)
            for xx in range(4):
                ylsrc[xx] = decode_late(1 - yl, xx, tl.at[0])
            ylcopy = remote(ylsrc, ylrx, yls, ylr, y_peer)
            for xx in range(4):
                xlsrc[xx] = decode_late(yl, xx, tl.at[0])
        if s == 12:
            ylcopy.wait()
            for xx in range(4):
                xlsrc[xx] = xlsrc[xx] + ylrx[xx]
            xlcopies = [
                remote(xlsrc.at[lax.rem(x + d, 4)], xlrx.at[k], xls.at[k], xlr.at[k], along_x(d))
                for k, d in enumerate((2, 1, 3))
            ]
    late_total = xlsrc[x]
    for k, copy in enumerate(xlcopies):
        copy.wait()
        late_total = late_total + xlrx[k]
    total = jnp.concatenate([total, late_total], axis=0)
    grad = total * (1.0 / (NX * NY * NZ))
    gz[z] = grad[:FIRST]
    cx[yl, x, 1] = grad[FIRST:]
    pl.semaphore_wait(heard.at[1], 4)
    partial = jnp.sum(grad * grad, axis=0, keepdims=True)
    for stage, ways in enumerate((ALONG_ZC, ALONG_YX)):
        first = stage * len(ALONG_ZC)
        sq[stage] = partial
        copies = [
            remote(sq.at[stage], ar_rx.at[first + i], qs.at[first + i], qr.at[first + i], partner(way))
            for i, way in enumerate(ways)
        ]
        if stage == 0:
            gcopies = spread(gz, gs, gr)
            acopies = pass_on(az, as_, ar, acopies)
            late = [
                remote(
                    cx.at[yl, x], cx.at[yl, x], cs.at[i], cr.at[i],
                    device(lax.rem(x + d, 4), (1 - yl) if other else yl, z),
                )
                for i, (other, d) in enumerate(((1, 2), (1, 1), (1, 3), (1, 0), (0, 2), (0, 1), (0, 3)))
            ]
            grad_out[...] = grad
        else:
            gcopies = pass_on(gz, gs, gr, gcopies)
        for copy in copies:
            copy.wait()
        partial = partial + jnp.sum(ar_rx[first : first + len(ways)], axis=0)
    mean = jnp.sum(partial, axis=1, keepdims=True) * (1.0 / (512 * ROWS * 128))
    inputs[3].wait()
    factor = jnp.minimum(1.0, clip_v[...] / jnp.sqrt(mean + 1e-06))
    factor_out[...] = jnp.broadcast_to(factor, (8, 128))
    step = 1.33 * factor
    for copy in late:
        copy.wait()
    for yy in range(NY):
        for xx in range(NX):
            nbc[yy, xx] = (cx[yy, xx, 0] - step * cx[yy, xx, 1]).astype(BF16)
    here = gathered.at[z, :, :, pl.ds(FIRST, LAST)]
    done = [
        remote(nbc, here, ds_.at[i], dr.at[i], along_z(d)) for i, d in enumerate((4, 3, 5, 2, 6, 1, 7))
    ]
    late_own = pltpu.make_async_copy(nbc, here, late_sem)
    late_own.start()
    for copy in acopies + gcopies:
        copy.wait()

    items_a = ((0, 0, FIRST), (1, 0, FIRST), (2, 0, FIRST), (3, 0, HALF))
    items_b = ((4, 0, FIRST), (5, 0, FIRST), (6, 0, FIRST), (3, HALF, FIRST - HALF), (7, 0, FIRST))
    counter = [0]

    def base_to(item, yy, xx, to, first=False):
        n = counter[0]
        counter[0] += 1
        zi, row, rows = item
        block = gathered.at[zi, yy, xx, pl.ds(row, rows)]
        return remote(nb.at[zi, pl.ds(row, rows)] if first else block, block, bs.at[n], br.at[n], to)

    right, left = along_x(1), along_x(3)
    x_left, x_right = lax.rem(x + 3, 4), lax.rem(x + 1, 4)
    x_far = lax.rem(x + 2, 4)

    def both_ways(item, yy, first=False):
        return base_to(item, yy, x, right, first), base_to(item, yy, x, left, first)

    def further(item, yy, way):
        return base_to(item, yy, x_left, right) if way else base_to(item, yy, x_right, left)

    a_x, b_y = [], []
    for i in range(5):
        for zi in ((0, 4), (1, 5), (2, 6), (3,), (7,))[i]:
            nb[zi] = (az[zi] - step * gz[zi]).astype(BF16)
        b_y.append(base_to(items_b[i], yl, x, y_peer, True))
        if i < 4:
            a_x.append(both_ways(items_a[i], yl, True))
    whole = pltpu.make_async_copy(nb, gathered.at[:, yl, x, pl.ds(0, FIRST)], own_sem)
    whole.start()
    b_x, b_x2, a_far = [], [], []
    for i in range(5):
        if i < 4:
            done.append(base_to(items_a[i], yl, x, y_peer, True))
        b_x.append(both_ways(items_b[i], yl, True))
    for i in range(5):
        if i < 4:
            for copy in a_x[i]:
                copy.wait()
            a_far.append(further(items_a[i], yl, i % 2 == 0))
            done.append(base_to(items_a[i], yl, x_left, y_peer))
            done.append(base_to(items_a[i], yl, x_right, y_peer))
        b_y[i].wait()
        b_x2.append(both_ways(items_b[i], 1 - yl))
    for i in range(5):
        if i < 4:
            a_far[i].wait()
            done.append(base_to(items_a[i], yl, x_far, y_peer))
        for yy, pair, way in ((yl, b_x[i], i % 2 == 1), (1 - yl, b_x2[i], i % 2 == 0)):
            for copy in pair:
                copy.wait()
            done.append(further(items_b[i], yy, way))
    late_own.wait()
    whole.wait()
    for copy in done:
        copy.wait()


def finish_kernel(
    gathered, grad, factor, master, momentum,
    base, new_master, new_momentum,
    rows, master_v, momentum_v, nm_v, nmom_v, small_sem, out_sem,
):
    smalls = [
        pltpu.make_async_copy(here, there, small_sem.at[i])
        for i, (here, there) in enumerate(
            ((master, master_v), (momentum, momentum_v))
        )
    ]
    for copy in smalls:
        copy.start()
    outs = []
    for n in range(4):
        i, h = n // 2, n % 2
        for j in range(0, ROWS, 16):
            turned = jnp.swapaxes(gathered[16 * i : 16 * (i + 1), h, j : j + 16, :], 0, 1)
            for k in range(16):
                rows[i, h, :, 128 * (j + k) : 128 * (j + k + 1)] = turned[k]
        out = pltpu.make_async_copy(
            rows.at[i, h], base.at[pl.ds(16 * i, 16), pl.ds(h * (FF // 2), FF // 2)], out_sem.at[n]
        )
        out.start()
        outs.append(out)
    for copy in smalls:
        copy.wait()
    scaled = factor[0:1, 0:1] * grad[...]
    moved = 0.9 * momentum_v[...] + scaled
    nmom_v[...] = moved
    nm_v[...] = master_v[...] - 0.7 * (scaled + 0.9 * moved)
    outs += [
        pltpu.make_async_copy(nm_v, new_master, out_sem.at[4]),
        pltpu.make_async_copy(nmom_v, new_momentum, out_sem.at[5]),
    ]
    for copy in outs[4:]:
        copy.start()
    for copy in outs:
        copy.wait()


def per_device(deltas, scales, clip_level, master, momentum):
    vmem, anywhere = pl.BlockSpec(memory_space=pltpu.VMEM), pl.BlockSpec(memory_space=pl.ANY)
    dma = pltpu.SemaphoreType.DMA
    deltas, scales, master, momentum = (
        pltpu.with_memory_space_constraint(a, pltpu.HBM)
        for a in (deltas.reshape(NZ * NY, NX, ROWS, 128), scales, master, momentum)
    )
    gathered, grad, factor = pl.pallas_call(
        kernel,
        out_shape=(
            pltpu.VMEM((NZ, NY, NX, ROWS, 128), BF16),
            pltpu.VMEM((ROWS, 128), F32),
            pltpu.VMEM((8, 128), F32),
        ),
        in_specs=[anywhere] * 5,
        out_specs=(vmem, vmem, vmem),
        scratch_shapes=[
            pltpu.VMEM((1, NZ * NY * NX * ROWS), BF16),
            pltpu.VMEM((1, 1), F32),
            pltpu.VMEM((ROWS, 128), F32),
            pltpu.VMEM((ROWS, 128), F32),
            pltpu.VMEM((NZ * NY, NX, PAD, 128), BF16),
            pltpu.VMEM((NX, NZ * NY, 128), F32),
            pltpu.VMEM((NX, NZ * NY, 128), BF16),
            pltpu.VMEM((NX, NZ * NY, 128), BF16),
            pltpu.VMEM((NX, NZ * NY, 128), F32),
            pltpu.VMEM((NZ, EARLY, 128), F32),
            pltpu.VMEM((NZ, EARLY, 128), F32),
            pltpu.VMEM((NZ - 1, EARLY, 128), F32),
            pltpu.VMEM((NZ - 1, EARLY, 128), F32),
            pltpu.VMEM((NZ, FIRST, 128), F32),
            pltpu.VMEM((NZ, FIRST, 128), F32),
            pltpu.VMEM((NZ, FIRST, 128), BF16),
            pltpu.VMEM((NY, NX, 2, LAST, 128), F32),
            pltpu.VMEM((NY, NX, LAST, 128), BF16),
            pltpu.VMEM((NY, NX, NZ * LATE, 128), BF16),
            pltpu.VMEM((NZ, NY * NX, 128), F32),
            pltpu.VMEM((NZ, NY * NX, 128), F32),
            pltpu.VMEM((NX, LATE, 128), F32),
            pltpu.VMEM((NX, LATE, 128), F32),
            pltpu.VMEM((NX, LATE, 128), F32),
            pltpu.VMEM((NX - 1, LATE, 128), F32),
            pltpu.VMEM((2, 1, 128), F32),
            pltpu.VMEM((46, 1, 128), F32),
            pltpu.SemaphoreType.REGULAR((2,)),
            dma,
            dma,
            dma((4,)),
            dma((16, 3)), dma((16, 3)),
            dma((3,)), dma((3,)),
            dma((8,)), dma((8,)),
            dma((7,)), dma((7,)),
            dma((8,)), dma((8,)),
            dma((8,)), dma((8,)),
            dma((7,)), dma((7,)),
            dma((46,)), dma((46,)),
            dma((63,)), dma((63,)),
            dma((7,)), dma((7,)),
            dma((7,)), dma((7,)),
            dma((7,)), dma((7,)),
            dma, dma,
            dma((3,)), dma((3,)),
        ],
        compiler_params=pltpu.CompilerParams(
            collective_id=0, has_side_effects=True, vmem_limit_bytes=40 * 2**20
        ),
    )(
        deltas, scales, clip_level.reshape(1, 1), master, momentum
    )
    half = FF // 2
    return pl.pallas_call(
        finish_kernel,
        out_shape=(
            jax.ShapeDtypeStruct((32, FF), BF16),
            jax.ShapeDtypeStruct((ROWS, 128), F32),
            jax.ShapeDtypeStruct((ROWS, 128), F32),
        ),
        in_specs=[vmem] * 3 + [anywhere] * 2,
        out_specs=(anywhere,) * 3,
        scratch_shapes=[
            pltpu.VMEM((2, 2, 16, half), BF16),
            pltpu.VMEM((ROWS, 128), F32),
            pltpu.VMEM((ROWS, 128), F32),
            pltpu.VMEM((ROWS, 128), F32),
            pltpu.VMEM((ROWS, 128), F32),
            dma((2,)), dma((6,)),
        ],
        compiler_params=pltpu.CompilerParams(vmem_limit_bytes=40 * 2**20),
    )(gathered.reshape(32, 2, ROWS, 128), grad, factor, master, momentum)


def solution(mesh):
    fr = ("fsdp", "rep")
    in_specs = (P("rep", "fsdp", None), P("rep", "fsdp"), P(), P(fr, None), P(fr, None))
    out_specs = (P("fsdp", None), P(fr, None), P(fr, None))
    return jax.shard_map(
        per_device, mesh=mesh, in_specs=in_specs, out_specs=out_specs, check_vma=False
    )
```
